256 devices in a mesh: stream: 4 (over x), seq: 64 (over z, y, core).
Axes of the slice: x: 4, y: 4, z: 8, core: 2. Of those that a mesh axis runs over, the one named last changes fastest.
Arguments:
- inputs: bfloat16 [4, 8192, 2048], P('stream', 'seq'), may hold values from -16 to 16
- cotangent: bfloat16 [4, 8192, 2048], P('stream', 'seq'), may hold values from -6 to 6
- lengths: int32 [4, 4], P('stream'), may hold values from 1 to 6144, 8192 in all within a row
- angles: float32 [2, 2048], replicated, may hold values from -3.140625 to 3.140625
- mix: float32 [14, 2048], replicated, may hold values from -1.5 to 1.5
- weight: bfloat16 [2048, 2048], replicated, may hold values from -0.125 to 0.125
Outputs:
- output: bfloat16 [4, 8192, 2048], P('stream', 'seq')
- input_grad: bfloat16 [4, 8192, 2048], P('stream', 'seq')
- weight_grad: float32 [2048, 2048], P('seq')
- angle_grad: float32 [2, 2048], replicated
- mix_grad: float32 [14, 2048], replicated
The draws below stay inside these ranges and needn't reach their ends.
Inputs may be any that keep to these rules, and one draw needn't show every extreme that they name: Each row holds the lengths of the 4 documents of one stream in time order; they sum to 8192, and the longest is exactly 6144.
All inputs are finite; a program needn't handle non-finite values.
Results may differ from the reference program's by a relative error of at most 0.012.
Values may be sent and summed in bfloat16 or wider, within the bound.
No kernel may reach another device: no remote copies, remote signals or barrier semaphores. Data moves between devices by JAX's collectives and lax.ppermute only.
A program may use at most 128 MiB of HBM per device.

```python
import math
import jax
import jax.numpy as jnp
import numpy as np
from jax import lax

C = 2048
SEGS = 4
STREAMS = 4
LENGTH = 8192
LEVELS = 13


def strengthened(drawn, stream_key, source, target, shards_of, factor):
    owner, partner = [(jnp.arange(drawn.shape[dim]) // (drawn.shape[dim] // shards_of)).reshape([-1 if axis == dim else 1 for axis in range(drawn.ndim)]) for dim in (source, target)]
    chosen = jax.random.permutation(stream_key, shards_of)[partner]
    strong = (owner == chosen) | (owner == (partner + shards_of // 2) % shards_of)
    return jnp.where(strong, factor * drawn, drawn)


def level_of(own_key, shape, pieces, low, top_value):
    gain, own = 1.0, jax.random.fold_in(own_key, 6)
    for axis_at, shards_of in pieces:
        steps = jnp.exp(jax.random.uniform(jax.random.fold_in(own, axis_at), (shards_of,), jnp.float32, low / len(pieces), top_value / len(pieces)))
        gain = gain * jnp.repeat(steps, shape[axis_at] // shards_of).reshape([-1 if axis == axis_at else 1 for axis in range(len(shape))])
    return gain


def profile(count, total, limit, lean):
    loads = [(1 << 20) // math.isqrt(grade ** lean) + 1 for grade in range(2, count + 1)]
    surplus, given = total - limit - (count - 1), [1] * (count - 1)
    while surplus > 0:
        free = [i for i in range(count - 1) if given[i] < limit]
        whole, budget = sum([loads[i] for i in free]), surplus
        for i in free:
            more = min(limit - given[i], max(1, budget * loads[i] // whole), surplus)
            given[i] = given[i] + more
            surplus = surplus - more
    return np.array([limit] + given)


def uneven_parts(key, count, total, limit, lean):
    if count == 2:
        one = jax.random.randint(key, (), max(1, total - limit), min(limit, total - 1) + 1)
        return jnp.stack([one, total - one])
    tallies = jnp.asarray(profile(count, total, limit, lean), jnp.int32)
    couples = (count - 1) // 2
    donor, sink = tallies[1:1 + 2 * couples:2], tallies[2:2 + 2 * couples:2]
    margin = jnp.minimum(donor - 1, limit - sink)
    passed = jax.random.randint(jax.random.fold_in(key, 1), (couples,), 0, 1 << 20) % (margin + 1)
    tallies = tallies.at[1:1 + 2 * couples:2].set(donor - passed).at[2:2 + 2 * couples:2].set(sink + passed)
    return tallies[jax.random.permutation(jax.random.fold_in(key, 2), count)]


def gaussian(key, dims, spread, bound, pieces=(), kind=jnp.bfloat16):
    array = spread * jax.random.normal(key, dims, jnp.float32)
    if pieces:
        array = array * level_of(key, dims, pieces, -0.22, 0.18)
    return jnp.clip(array, -bound, bound).astype(kind)


def bell_draw_with(own_key, extent, width, limit, cuts, heavy, kind=jnp.bfloat16):
    values = width * jax.random.normal(own_key, extent, jnp.float32)
    if cuts:
        values = values * level_of(own_key, extent, cuts, -0.22, 0.18)
    return jnp.clip(strengthened(values, jax.random.fold_in(own_key, 3), *heavy), -limit, limit).astype(kind)


def setup_inputs(seed: int = 0) -> dict:
    keys = jax.random.split(jax.random.key(seed), 7)
    inputs = bell_draw_with(keys[0], (STREAMS, LENGTH, C), 1.0, 16.0, ((0, 4), (1, 64)), (1, 2, 64, 4.0))
    cotangent = gaussian(keys[1], (STREAMS, LENGTH, C), 1.0, 6.0, ((0, 4), (1, 64)))
    lengths = jax.vmap(lambda own: uneven_parts(own, SEGS, LENGTH, LENGTH // 2 + LENGTH // 4, 0))(jax.random.split(keys[2], STREAMS)).reshape((STREAMS, SEGS)).astype(jnp.int32)
    angles = jnp.clip(jax.random.uniform(keys[3], (2, C), jnp.float32, -3.140625, 3.140625), -3.140625, 3.140625)
    mix = gaussian(keys[4], (LEVELS + 1, C), 0.3, 1.5, (), jnp.float32)
    weight = gaussian(keys[5], (C, C), C ** -0.5, 0.125)
    return dict(inputs=inputs, cotangent=cotangent, lengths=lengths, angles=angles, mix=mix, weight=weight)


def segment_start(lengths_row, times):
    ends = jnp.cumsum(lengths_row, dtype=jnp.int32)
    hits = jnp.where(ends[None, :] <= times[:, None], lengths_row[None, :], 0)
    return lax.optimization_barrier(jnp.sum(hits, axis=1, dtype=jnp.int32))

def tap_mask(times, start, dist):
    return (times - dist >= start).astype(jnp.float32)

def delay_rows(values, dist):
    filler = jnp.zeros((dist, values.shape[1]), values.dtype)
    return jnp.concatenate([filler, values[:values.shape[0] - dist]], axis=0)

def advance_rows(values, dist):
    filler = jnp.zeros((dist, values.shape[1]), values.dtype)
    return jnp.concatenate([values[dist:], filler], axis=0)

def one_stream(stream_in, stream_cot, stream_len, angles, mix, weight):
    cos_a = jnp.cos(angles[0])
    sin_a = jnp.sin(angles[0])
    cos_d = jnp.cos(angles[1])
    sin_d = jnp.sin(angles[1])
    times = jnp.arange(LENGTH, dtype=jnp.int32)
    start = segment_start(stream_len, times)
    current = stream_in
    stored = [current]
    mixed = jnp.zeros((LENGTH, C), jnp.float32)
    for level in range(LEVELS):
        dist = 2 ** level
        mask = tap_mask(times, start, dist)[:, None]
        shifted = delay_rows(current, dist).astype(jnp.float32) * mask
        plain = current.astype(jnp.float32)
        mixed = mixed + mix[level] * (cos_d * plain + sin_d * shifted)
        current = lax.optimization_barrier((cos_a * plain + sin_a * shifted).astype(jnp.bfloat16))
        stored.append(current)
    mixed = mixed + mix[LEVELS] * current.astype(jnp.float32)
    act = jax.nn.gelu(mixed).astype(jnp.bfloat16)
    output = jnp.dot(act, weight, preferred_element_type=jnp.float32).astype(jnp.bfloat16)
    act_grad = lax.optimization_barrier(jnp.dot(stream_cot, weight.T, preferred_element_type=jnp.float32).astype(jnp.bfloat16))
    unused, pull = jax.vjp(jax.nn.gelu, mixed)
    mixed_grad = lax.optimization_barrier(pull(act_grad.astype(jnp.float32))[0].astype(jnp.bfloat16))
    weight_term = lax.dot_general(act, stream_cot, (((0,), (0,)), ((), ())), preferred_element_type=jnp.float32)
    grad_full = mixed_grad.astype(jnp.float32)
    upper = mix[LEVELS] * grad_full
    mix_rows = [None] * (LEVELS + 1)
    mix_rows[LEVELS] = lax.optimization_barrier(jnp.sum(grad_full * stored[LEVELS].astype(jnp.float32), axis=0))
    theta = jnp.zeros((C,), jnp.float32)
    phi = jnp.zeros((C,), jnp.float32)
    carried = stored[0]
    for level in reversed(range(LEVELS)):
        dist = 2 ** level
        mask = tap_mask(times, start, dist)[:, None]
        plain = stored[level].astype(jnp.float32)
        shifted = delay_rows(stored[level], dist).astype(jnp.float32) * mask
        along = mix[level] * grad_full
        mix_rows[level] = lax.optimization_barrier(jnp.sum(grad_full * (cos_d * plain + sin_d * shifted), axis=0))
        theta = theta + lax.optimization_barrier(jnp.sum(upper * (cos_a * shifted - sin_a * plain), axis=0))
        phi = phi + lax.optimization_barrier(jnp.sum(along * (cos_d * shifted - sin_d * plain), axis=0))
        sent = lax.optimization_barrier((mask * (sin_a * upper + sin_d * along)).astype(jnp.bfloat16))
        back = advance_rows(sent, dist).astype(jnp.float32)
        carried = lax.optimization_barrier((cos_a * upper + cos_d * along + back).astype(jnp.bfloat16))
        upper = carried.astype(jnp.float32)
    return (output, carried, weight_term, jnp.stack([theta, phi]), jnp.stack(mix_rows))

def reference(inputs, cotangent, lengths, angles, mix, weight):

    def run(packed):
        return one_stream(packed[0], packed[1], packed[2], angles, mix, weight)
    output, input_grad, weight_terms, angle_terms, mix_terms = lax.map(run, (inputs, cotangent, lengths))
    factor = float(STREAMS * LENGTH) ** (-0.5)
    weight_grad = lax.optimization_barrier(jnp.sum(weight_terms, axis=0)) * factor
    angle_grad = lax.optimization_barrier(jnp.sum(angle_terms, axis=0)) * factor
    mix_grad = lax.optimization_barrier(jnp.sum(mix_terms, axis=0)) * factor
    return (output, input_grad, weight_grad, angle_grad, mix_grad)
```

```python
import functools
import math

import jax
import jax.numpy as jnp
from jax import lax
from jax.experimental import pallas as pl
from jax.experimental.pallas import tpu as pltpu
from jax.sharding import Mesh
from jax.sharding import PartitionSpec as P

F32 = jnp.float32
BF16 = jnp.bfloat16
ROWS = 2048
PAD = 1024
LEVELS = 13
CHUNK = 128
GELU_K = math.sqrt(2.0 / math.pi)
VMEM_LIMIT = 60000 * 1024


def swap_groups(tiles, width):
    count = len(tiles)
    lane = lax.broadcasted_iota(jnp.int32, tiles[0].shape, 1)
    bit = 1
    while bit < count:
        high = (lane // width) & bit != 0
        new = list(tiles)
        for t in range(count):
            if t & bit == 0:
                a, b = tiles[t], tiles[t | bit]
                new[t] = jnp.where(high, pltpu.roll(b, bit * width, 1), a)
                new[t | bit] = jnp.where(high, b, pltpu.roll(a, 128 - bit * width, 1))
        tiles = new
        bit *= 2
    return tiles


def row_order(inverse):
    i = lax.broadcasted_iota(jnp.int32, (128, 128), 0)
    k = lax.broadcasted_iota(jnp.int32, (128, 128), 1)
    if inverse:
        i, k = k, i
    return (k == 4 * (i % 32) + i // 32).astype(F32).astype(BF16)


def dot(a, b, dims):
    return lax.dot_general(a, b, (dims, ((), ())), preferred_element_type=F32)


def pack_kernel(x_ref, cot_ref, w_ref, out_ref):
    order = row_order(False)
    act_grad = dot(cot_ref[...], w_ref[...], ((1,), (1,))).astype(BF16)
    for at, block in ((0, x_ref[...]), (32, act_grad)):
        ordered = dot(order, block, ((1,), (0,)))
        for tile in range(block.shape[1] // 128):
            part = [ordered[32 * q : 32 * q + 32, 128 * tile : 128 * tile + 128] for q in range(4)]
            for jj, value in enumerate(swap_groups(part, 32)):
                out_ref[4 * tile + jj, at : at + 32, :] = value.astype(BF16)


def pack(x, cot, weight):
    width = 512
    return pl.pallas_call(
        pack_kernel,
        grid=(2048 // width,),
        in_specs=[
            pl.BlockSpec((128, width), lambda n: (0, n)),
            pl.BlockSpec((128, 2048), lambda n: (0, 0)),
            pl.BlockSpec((width, 2048), lambda n: (n, 0)),
        ],
        out_specs=pl.BlockSpec((width // 32, 64, 128), lambda n: (n, 0, 0)),
        out_shape=jax.ShapeDtypeStruct((64, 64, 128), BF16),
        name="pack",
    )(x, cot, weight)


def order_kernel(cot_ref, out_ref):
    out_ref[...] = dot(row_order(False), cot_ref[...], ((1,), (0,))).astype(BF16)


def order_rows(cot):
    return pl.pallas_call(
        order_kernel, out_shape=jax.ShapeDtypeStruct((128, 2048), BF16), name="order_rows"
    )(cot)


def cascade_kernel(len_ref, coef_ref, in_ref, out_ref, a_ref, pos_ref, mixed_ref, g_ref, u_ref, sum_ref):
    lane = lax.broadcasted_iota(jnp.int32, (CHUNK, 128), 1)
    cos_a, sin_a = jnp.cos(coef_ref[0:1, :]), jnp.sin(coef_ref[0:1, :])
    cos_d, sin_d = jnp.cos(coef_ref[1:2, :]), jnp.sin(coef_ref[1:2, :])
    mix = [coef_ref[2 + level : 3 + level, :] for level in range(LEVELS + 1)]
    sources = CHUNK // 32

    def fold(value):
        return jnp.sum(value.reshape(CHUNK // 8, 8, 128), axis=0)

    def start_up(n, carry):
        r0 = pl.multiple_of(n * CHUNK, CHUNK)
        row = lax.broadcasted_iota(jnp.int32, (CHUNK, 128), 0)
        time = 4 * (r0 + row) + lane // 32
        start = jnp.zeros((CHUNK, 128), jnp.int32)
        end = jnp.int32(0)
        for s in range(4):
            length = len_ref[0, s]
            end = end + length
            start = start + jnp.where(end <= time, length, 0)
        pos_ref[pl.ds(r0, CHUNK), :] = time - start
        got = in_ref[pl.ds(n * sources, sources), 0:32, :].astype(F32)
        a_ref[0, pl.ds(PAD + r0, CHUNK), :] = got.reshape(CHUNK, 128)
        return carry

    lax.fori_loop(0, ROWS // CHUNK, start_up, 0)
    pos_ref[pl.ds(ROWS, PAD), :] = jnp.full((PAD, 128), -1, jnp.int32)

    def behind(level, r0):
        dist = 2**level
        if dist >= 4:
            moved = a_ref[level, pl.ds(PAD + r0 - dist // 4, CHUNK), :]
        else:
            here = a_ref[level, pl.ds(PAD + r0, CHUNK), :]
            before = a_ref[level, pl.ds(PAD + r0 - 1, CHUNK), :]
            moved = pltpu.roll(jnp.where(lane >= 128 - 32 * dist, before, here), 32 * dist, 1)
        return jnp.where(pos_ref[pl.ds(r0, CHUNK), :] >= dist, moved, 0.0)

    for level in range(LEVELS):
        to_mix = mix[level] * cos_d
        to_mix_s = mix[level] * sin_d

        def forward(n, carry, level=level, to_mix=to_mix, to_mix_s=to_mix_s):
            r0 = pl.multiple_of(n * CHUNK, CHUNK)
            rows = pl.ds(r0, CHUNK)
            plain = a_ref[level, pl.ds(PAD + r0, CHUNK), :]
            shifted = behind(level, r0)
            term = to_mix * plain + to_mix_s * shifted
            mixed = term if level == 0 else mixed_ref[rows, :] + term
            above = cos_a * plain + sin_a * shifted
            if level < LEVELS - 1:
                mixed_ref[rows, :] = mixed
                a_ref[level + 1, pl.ds(PAD + r0, CHUNK), :] = above
                return carry
            z = mixed + mix[LEVELS] * above
            th = jnp.tanh(GELU_K * (z + 0.044715 * (z * z * z)))
            half = 0.5 * (1.0 + th)
            act = z * half
            slope = half + 0.5 * z * (1.0 - th * th) * (GELU_K * (1.0 + 3 * 0.044715 * (z * z)))
            blocks = pl.ds(n * sources, sources)
            act_grad = in_ref[blocks, 32:64, :].astype(F32).reshape(CHUNK, 128)
            g = (slope * act_grad).astype(BF16).astype(F32)
            out_ref[blocks, 0:32, :] = act.astype(BF16).reshape(sources, 32, 128)
            g_ref[rows, :] = g
            u_ref[1, rows, :] = mix[LEVELS] * g
            return carry + fold(g * above)

        zero = jnp.zeros((8, 128), F32)
        if level < LEVELS - 1:
            lax.fori_loop(0, ROWS // CHUNK, forward, 0)
        else:
            top = lax.fori_loop(0, ROWS // CHUNK, forward, zero)

    def over_q(value):
        row = jnp.sum(value, axis=0, keepdims=True)
        row = row + pltpu.roll(row, 32, 1)
        return row + pltpu.roll(row, 64, 1)

    sum_ref[15:16, :] = over_q(top)
    sum_ua = jnp.zeros((8, 128), F32)
    sum_us = jnp.zeros((8, 128), F32)
    phi = jnp.zeros((1, 128), F32)
    for level in reversed(range(LEVELS)):
        dist = 2**level
        source, target = (1, 0) if level % 2 == 0 else (0, 1)
        from_g = mix[level] * cos_d
        from_g_s = mix[level] * sin_d

        def backward(n, carry, level=level, dist=dist, source=source, target=target, from_g=from_g, from_g_s=from_g_s):
            ua, us, ga, gs = carry
            r0 = pl.multiple_of(n * CHUNK, CHUNK)
            rows = pl.ds(r0, CHUNK)
            u, g = u_ref[source, rows, :], g_ref[rows, :]
            if dist >= 4:
                later = pl.ds(r0 + dist // 4, CHUNK)
                u_on, g_on, pos = u_ref[source, later, :], g_ref[later, :], pos_ref[later, :]
            else:
                later = pl.ds(r0 + 1, CHUNK)

                def ahead(here, there):
                    return pltpu.roll(jnp.where(lane < 32 * dist, there, here), 128 - 32 * dist, 1)

                u_on = ahead(u, u_ref[source, later, :])
                g_on = ahead(g, g_ref[later, :])
                pos = ahead(pos_ref[rows, :], pos_ref[later, :])
            keep = pos >= dist
            u_on = jnp.where(keep, u_on, 0.0)
            g_on = jnp.where(keep, g_on, 0.0)
            new = (cos_a * u + from_g * g) + (sin_a * u_on + from_g_s * g_on)
            plain = a_ref[level, pl.ds(PAD + r0, CHUNK), :]
            if level > 0:
                u_ref[target, rows, :] = new
            else:
                blocks = pl.ds(n * sources, sources)
                out_ref[blocks, 32:64, :] = new.astype(BF16).reshape(sources, 32, 128)
            return (
                ua + fold(u * plain),
                us + fold(u_on * plain),
                ga + fold(g * plain),
                gs + fold(g_on * plain),
            )

        zero = jnp.zeros((8, 128), F32)
        sum_ua, sum_us, ga, gs = lax.fori_loop(
            0, ROWS // CHUNK, backward, (sum_ua, sum_us, zero, zero)
        )
        ga, gs = over_q(ga), over_q(gs)
        sum_ref[2 + level : 3 + level, :] = cos_d * ga + sin_d * gs
        phi = phi + mix[level] * (cos_d * gs - sin_d * ga)
    sum_ref[0:1, :] = cos_a * over_q(sum_us) - sin_a * over_q(sum_ua)
    sum_ref[1:2, :] = phi
    group = lax.broadcasted_iota(jnp.int32, (4, 128), 1) // 32
    packed = jnp.zeros((4, 128), F32)
    for b in range(4):
        packed = jnp.where(group == b, sum_ref[4 * b : 4 * b + 4, :], packed)
    high = packed.astype(BF16).astype(F32)
    both = jnp.concatenate([high, packed - high], axis=0).astype(BF16)
    out_ref[:, 64:72, :] = jnp.broadcast_to(both[None], (64, 8, 128))


def cascade(lengths, coef, received):
    return pl.pallas_call(
        cascade_kernel,
        in_specs=[
            pl.BlockSpec(memory_space=pltpu.SMEM),
            pl.BlockSpec(memory_space=pltpu.VMEM),
            pl.BlockSpec(memory_space=pltpu.VMEM),
        ],
        out_specs=pl.BlockSpec(memory_space=pltpu.VMEM),
        out_shape=jax.ShapeDtypeStruct((64, 72, 128), BF16),
        scratch_shapes=[
            pltpu.VMEM((LEVELS, PAD + ROWS, 128), F32),
            pltpu.VMEM((ROWS + PAD, 128), jnp.int32),
            pltpu.VMEM((ROWS, 128), F32),
            pltpu.VMEM((ROWS + PAD, 128), F32),
            pltpu.VMEM((2, ROWS + PAD, 128), F32),
            pltpu.VMEM((16, 128), F32),
        ],
        compiler_params=pltpu.CompilerParams(vmem_limit_bytes=VMEM_LIMIT),
        name="cascade",
    )(lengths, coef, received)


def unpack_kernel(place_ref, in_ref, act_ref, grad_ref, send_ref, sums_ref):
    x, c = place_ref[0], place_ref[1]
    order = row_order(True)
    for tile in range(16):
        lanes = slice(128 * tile, 128 * tile + 128)
        for at, out in ((0, act_ref), (32, grad_ref)):
            part = [in_ref[4 * tile + jj, at : at + 32, :].astype(F32) for jj in range(4)]
            rows = jnp.concatenate(swap_groups(part, 32), axis=0).astype(BF16)
            out[:, lanes] = dot(order, rows, ((1,), (0,))).astype(BF16)
        part = []
        for jj in range(4):
            both = in_ref[4 * tile + jj, 64:72, :].astype(F32)
            part.append(both[0:4] + both[4:8])
        for b, value in enumerate(swap_groups(part, 32)):
            sums_ref[4 * b : 4 * b + 4, lanes] = value
    for half in range(2):
        for core in range(2):
            other = jnp.where(c == core, 0, 1)
            for chunk in range(2):
                part = [
                    in_ref[2 * (16 * half + k) + core, 16 * chunk : 16 * chunk + 16, :].astype(F32)
                    for k in range(16)
                ]
                for at, value in enumerate(swap_groups(part, 8)):
                    q, to = at // 4, at % 4
                    step = lax.rem(to - x + 4, 4)
                    row = 32 * q + 16 * chunk
                    send_ref[step, other, row : row + 16, 128 * half : 128 * half + 128] = value.astype(BF16)


def unpack(place, received):
    vmem = pl.BlockSpec(memory_space=pltpu.VMEM)
    return pl.pallas_call(
        unpack_kernel,
        in_specs=[pl.BlockSpec(memory_space=pltpu.SMEM), vmem],
        out_specs=[vmem] * 4,
        out_shape=[
            jax.ShapeDtypeStruct((128, 2048), BF16),
            jax.ShapeDtypeStruct((128, 2048), BF16),
            jax.ShapeDtypeStruct((4, 2, 128, 256), BF16),
            jax.ShapeDtypeStruct((16, 2048), F32),
        ],
        compiler_params=pltpu.CompilerParams(vmem_limit_bytes=VMEM_LIMIT),
        name="unpack",
    )(place, received)


def outer_kernel(a0, a1, a2, a3, a_far, c_near, c_far, out_ref):
    total = dot(a_far[...].reshape(512, 256), c_far[...].reshape(512, -1), ((0,), (0,)))
    for at, ref in enumerate((a0, a1, a2, a3)):
        total = total + dot(ref[0], c_near[at], ((0,), (0,)))
    out_ref[...] = total.astype(BF16)


def outer(acts, act_far, cot_near, cot_far):
    width = 512
    whole = pl.BlockSpec((2, 128, 256), lambda n: (0, 0, 0))
    part = pl.BlockSpec((4, 128, width), lambda n: (0, 0, n))
    return pl.pallas_call(
        outer_kernel,
        grid=(2048 // width,),
        in_specs=[whole] * 4 + [pl.BlockSpec((4, 128, 256), lambda n: (0, 0, 0)), part, part],
        out_specs=pl.BlockSpec((256, width), lambda n: (0, n)),
        out_shape=jax.ShapeDtypeStruct((256, 2048), BF16),
        name="outer",
    )(*acts, act_far, cot_near, cot_far)


def gather_kernel(place_ref, in_ref, sums_ref, out_ref, *, factor):
    total = jnp.sum(in_ref[...].astype(F32), axis=0) * factor
    for slot in range(4):
        out_ref[8 * slot : 8 * slot + 8, :] = jnp.where(place_ref[0] == slot, total, 0.0)
    out_ref[32:48, :] = sums_ref[...] * factor


def gather(place, received, sums, factor):
    vmem = pl.BlockSpec(memory_space=pltpu.VMEM)
    return pl.pallas_call(
        functools.partial(gather_kernel, factor=factor),
        in_specs=[pl.BlockSpec(memory_space=pltpu.SMEM), vmem, vmem],
        out_specs=vmem,
        out_shape=jax.ShapeDtypeStruct((48, 2048), F32),
        name="gather",
    )(place, received, sums)


def along_x(block, step):
    return lax.ppermute(block, "x", [(i, (i + step) % 4) for i in range(4)])


def other_core(block):
    return lax.ppermute(block, "c", [(0, 1), (1, 0)])


def body(inputs, cotangent, lengths, angles, mix, weight):
    x, cot = inputs[0], cotangent[0]
    seq = ("z", "y", "c")
    place = jnp.stack([lax.axis_index("x"), lax.axis_index("c")]).astype(jnp.int32)
    factor = float(4 * 8192) ** (-0.5)

    cot_rows = order_rows(cot)
    cot_near = jnp.stack([cot_rows] + [along_x(cot_rows, step) for step in (1, 2, 3)])
    cot_far = other_core(cot_near)

    coef = lax.dynamic_slice_in_dim(
        jnp.concatenate([angles, mix], axis=0), 32 * lax.axis_index(seq), 32, axis=1
    )
    coef = jnp.tile(coef, (1, 4))

    packed = pack(x, cot, weight)
    received = lax.all_to_all(packed, seq, split_axis=0, concat_axis=0, tiled=True)
    done = cascade(lengths, coef, received)
    back = lax.all_to_all(done, seq, split_axis=0, concat_axis=0, tiled=True)
    act, input_grad, send, sums = unpack(place, back)

    acts = [send[0]] + [along_x(send[step], step) for step in (1, 2, 3)]
    act_far = other_core(jnp.stack([block[1] for block in acts]))
    output = jnp.dot(act, weight, preferred_element_type=F32).astype(BF16)
    partial = outer(acts, act_far, cot_near, cot_far)
    pieces = lax.all_to_all(
        partial.reshape(32, 8, 2048), ("z", "y"), split_axis=0, concat_axis=0, tiled=True
    )
    total = lax.psum(gather(place, pieces, sums, factor), "x")
    return output[None], input_grad[None], total[:32], total[32:34], total[34:48]


def solution(mesh):
    grid = Mesh(mesh.devices.reshape(4, 8, 4, 2), ("x", "z", "y", "c"))
    seq = ("z", "y", "c")
    split = P("x", seq, None)
    in_specs = (split, split, P("x", None), P(), P(), P())
    out_specs = (split, split, P(seq, None), P(), P())
    return jax.shard_map(body, mesh=grid, in_specs=in_specs, out_specs=out_specs, check_vma=False)
```

```python
import functools
import math

import jax
import jax.numpy as jnp
from jax import lax
from jax.experimental import pallas as pl
from jax.experimental.pallas import tpu as pltpu
from jax.sharding import Mesh
from jax.sharding import PartitionSpec as P

F32 = jnp.float32
BF16 = jnp.bfloat16
ROWS = 2048
PAD = 1024
LEVELS = 13
CHUNK = 128
GELU_K = math.sqrt(2.0 / math.pi)
LARGE = pltpu.CompilerParams(vmem_limit_bytes=32 << 20)
SMALL = pltpu.CompilerParams(vmem_limit_bytes=12 << 20)


def swap_groups(tiles, width):
    count = len(tiles)
    lane = lax.broadcasted_iota(jnp.int32, tiles[0].shape, 1)
    bit = 1
    while bit < count:
        high = (lane // width) & bit != 0
        new = list(tiles)
        for t in range(count):
            if t & bit == 0:
                a, b = tiles[t], tiles[t | bit]
                new[t] = jnp.where(high, pltpu.roll(b, bit * width, 1), a)
                new[t | bit] = jnp.where(high, b, pltpu.roll(a, 128 - bit * width, 1))
        tiles = new
        bit *= 2
    return tiles


def row_order(inverse):
    i = lax.broadcasted_iota(jnp.int32, (128, 128), 0)
    k = lax.broadcasted_iota(jnp.int32, (128, 128), 1)
    if inverse:
        i, k = k, i
    return (k == 4 * (i % 32) + i // 32).astype(F32).astype(BF16)


def dot(a, b, dims):
    return lax.dot_general(a, b, (dims, ((), ())), preferred_element_type=F32)


def pack_kernel(x_ref, cot_ref, w_ref, out_ref):
    order = row_order(False)
    act_grad = dot(cot_ref[...], w_ref[...], ((1,), (1,))).astype(BF16)
    for at, block in ((0, x_ref[...]), (32, act_grad)):
        ordered = dot(order, block, ((1,), (0,)))
        for tile in range(block.shape[1] // 128):
            part = [ordered[32 * q : 32 * q + 32, 128 * tile : 128 * tile + 128] for q in range(4)]
            for jj, value in enumerate(swap_groups(part, 32)):
                out_ref[4 * tile + jj, at : at + 32, :] = value.astype(BF16)


def pack(x, cot, weight):
    width = 512
    return pl.pallas_call(
        pack_kernel,
        grid=(2048 // width,),
        in_specs=[
            pl.BlockSpec((128, width), lambda n: (0, n)),
            pl.BlockSpec((128, 2048), lambda n: (0, 0)),
            pl.BlockSpec((width, 2048), lambda n: (n, 0)),
        ],
        out_specs=pl.BlockSpec((width // 32, 64, 128), lambda n: (n, 0, 0)),
        out_shape=jax.ShapeDtypeStruct((64, 64, 128), BF16),
        cost_estimate=pl.CostEstimate(flops=2**30, bytes_accessed=2**23, transcendentals=0),
        name="pack",
    )(x, cot, weight)


def filters(coef_ref):
    cos_a, sin_a = jnp.cos(coef_ref[0:1, :]), jnp.sin(coef_ref[0:1, :])
    cos_d, sin_d = jnp.cos(coef_ref[1:2, :]), jnp.sin(coef_ref[1:2, :])
    mix = [coef_ref[2 + level : 3 + level, :] for level in range(LEVELS + 1)]
    return cos_a, sin_a, cos_d, sin_d, mix


def positions(len_ref, r0):
    row = lax.broadcasted_iota(jnp.int32, (CHUNK, 128), 0)
    lane = lax.broadcasted_iota(jnp.int32, (CHUNK, 128), 1)
    time = 4 * (r0 + row) + lane // 32
    start = jnp.zeros((CHUNK, 128), jnp.int32)
    end = jnp.int32(0)
    for s in range(4):
        length = len_ref[0, s]
        end = end + length
        start = start + jnp.where(end <= time, length, 0)
    return time - start


def forward_kernel(len_ref, coef_ref, in_ref, act_ref, mixed_ref, keep_ref, a_ref, pos_ref, sems):
    lane = lax.broadcasted_iota(jnp.int32, (CHUNK, 128), 1)
    cos_a, sin_a, cos_d, sin_d, mix = filters(coef_ref)
    sources = CHUNK // 32

    def start_up(n, carry):
        r0 = pl.multiple_of(n * CHUNK, CHUNK)
        pos_ref[pl.ds(r0, CHUNK), :] = positions(len_ref, r0)
        got = in_ref[pl.ds(n * sources, sources), 0:32, :].astype(F32)
        a_ref[0, pl.ds(PAD + r0, CHUNK), :] = got.reshape(CHUNK, 128)
        return carry

    def save(level):
        return pltpu.make_async_copy(
            a_ref.at[level, pl.ds(PAD, ROWS)], keep_ref.at[level], sems.at[level]
        )

    lax.fori_loop(0, ROWS // CHUNK, start_up, 0)
    save(0).start()

    def behind(level, r0):
        dist = 2**level
        if dist >= 4:
            moved = a_ref[level, pl.ds(PAD + r0 - dist // 4, CHUNK), :]
        else:
            here = a_ref[level, pl.ds(PAD + r0, CHUNK), :]
            before = a_ref[level, pl.ds(PAD + r0 - 1, CHUNK), :]
            moved = pltpu.roll(jnp.where(lane >= 128 - 32 * dist, before, here), 32 * dist, 1)
        return jnp.where(pos_ref[pl.ds(r0, CHUNK), :] >= dist, moved, 0.0)

    for level in range(LEVELS):
        to_mix = mix[level] * cos_d
        to_mix_s = mix[level] * sin_d

        def step(n, carry, level=level, to_mix=to_mix, to_mix_s=to_mix_s):
            r0 = pl.multiple_of(n * CHUNK, CHUNK)
            rows = pl.ds(r0, CHUNK)
            plain = a_ref[level, pl.ds(PAD + r0, CHUNK), :]
            shifted = behind(level, r0)
            term = to_mix * plain + to_mix_s * shifted
            mixed = term if level == 0 else mixed_ref[rows, :] + term
            above = cos_a * plain + sin_a * shifted
            a_ref[level + 1, pl.ds(PAD + r0, CHUNK), :] = above
            if level == LEVELS - 1:
                mixed = mixed + mix[LEVELS] * above
                th = jnp.tanh(GELU_K * (mixed + 0.044715 * (mixed * mixed * mixed)))
                act = mixed * (0.5 * (1.0 + th))
                blocks = pl.ds(n * sources, sources)
                act_ref[blocks] = act.astype(BF16).reshape(sources, 32, 128)
            mixed_ref[rows, :] = mixed
            return carry

        lax.fori_loop(0, ROWS // CHUNK, step, 0)
        save(level + 1).start()
    for level in range(LEVELS + 1):
        save(level).wait()


def forward(lengths, coef, received):
    vmem = pl.BlockSpec(memory_space=pltpu.VMEM)
    return pl.pallas_call(
        forward_kernel,
        in_specs=[pl.BlockSpec(memory_space=pltpu.SMEM), vmem, vmem],
        out_specs=[vmem, vmem, pl.BlockSpec(memory_space=pltpu.HBM)],
        out_shape=[
            jax.ShapeDtypeStruct((64, 32, 128), BF16),
            jax.ShapeDtypeStruct((ROWS, 128), F32),
            jax.ShapeDtypeStruct((LEVELS + 1, ROWS, 128), F32),
        ],
        scratch_shapes=[
            pltpu.VMEM((LEVELS + 1, PAD + ROWS, 128), F32),
            pltpu.VMEM((ROWS, 128), jnp.int32),
            pltpu.SemaphoreType.DMA((LEVELS + 1,)),
        ],
        compiler_params=LARGE,
        cost_estimate=pl.CostEstimate(flops=10**8, bytes_accessed=2**25, transcendentals=2**18),
        name="forward",
    )(lengths, coef, received)


def backward_kernel(len_ref, coef_ref, in_ref, mixed_ref, keep_ref, out_ref, a_ref, pos_ref, g_ref, u_ref, sum_ref, sems):
    lane = lax.broadcasted_iota(jnp.int32, (CHUNK, 128), 1)
    cos_a, sin_a, cos_d, sin_d, mix = filters(coef_ref)
    sources = CHUNK // 32

    def load(level):
        return pltpu.make_async_copy(keep_ref.at[level], a_ref.at[level], sems.at[level])

    for level in reversed(range(LEVELS + 1)):
        load(level).start()

    def fold(value):
        return jnp.sum(value.reshape(CHUNK // 8, 8, 128), axis=0)

    def over_q(value):
        row = jnp.sum(value, axis=0, keepdims=True)
        row = row + pltpu.roll(row, 32, 1)
        return row + pltpu.roll(row, 64, 1)

    zero = jnp.zeros((8, 128), F32)
    load(LEVELS).wait()

    def start_up(n, carry):
        r0 = pl.multiple_of(n * CHUNK, CHUNK)
        rows = pl.ds(r0, CHUNK)
        pos_ref[rows, :] = positions(len_ref, r0)
        z = mixed_ref[rows, :]
        th = jnp.tanh(GELU_K * (z + 0.044715 * (z * z * z)))
        half = 0.5 * (1.0 + th)
        slope = half + 0.5 * z * (1.0 - th * th) * (GELU_K * (1.0 + 3 * 0.044715 * (z * z)))
        act_grad = in_ref[pl.ds(n * sources, sources), 32:64, :].astype(F32).reshape(CHUNK, 128)
        g = (slope * act_grad).astype(BF16).astype(F32)
        g_ref[rows, :] = g
        u_ref[1, rows, :] = mix[LEVELS] * g
        return carry + fold(g * a_ref[LEVELS, rows, :])

    sum_ref[15:16, :] = over_q(lax.fori_loop(0, ROWS // CHUNK, start_up, zero))
    pos_ref[pl.ds(ROWS, PAD), :] = jnp.full((PAD, 128), -1, jnp.int32)

    sum_ua, sum_us = zero, zero
    phi = jnp.zeros((1, 128), F32)
    for level in reversed(range(LEVELS)):
        dist = 2**level
        source, target = (1, 0) if level % 2 == 0 else (0, 1)
        from_g = mix[level] * cos_d
        from_g_s = mix[level] * sin_d
        load(level).wait()

        def step(n, carry, level=level, dist=dist, source=source, target=target, from_g=from_g, from_g_s=from_g_s):
            ua, us, ga, gs = carry
            r0 = pl.multiple_of(n * CHUNK, CHUNK)
            rows = pl.ds(r0, CHUNK)
            u, g = u_ref[source, rows, :], g_ref[rows, :]
            if dist >= 4:
                later = pl.ds(r0 + dist // 4, CHUNK)
                u_on, g_on, pos = u_ref[source, later, :], g_ref[later, :], pos_ref[later, :]
            else:
                later = pl.ds(r0 + 1, CHUNK)

                def ahead(here, there):
                    return pltpu.roll(jnp.where(lane < 32 * dist, there, here), 128 - 32 * dist, 1)

                u_on = ahead(u, u_ref[source, later, :])
                g_on = ahead(g, g_ref[later, :])
                pos = ahead(pos_ref[rows, :], pos_ref[later, :])
            keep = pos >= dist
            u_on = jnp.where(keep, u_on, 0.0)
            g_on = jnp.where(keep, g_on, 0.0)
            new = (cos_a * u + from_g * g) + (sin_a * u_on + from_g_s * g_on)
            plain = a_ref[level, rows, :]
            if level > 0:
                u_ref[target, rows, :] = new
            else:
                blocks = pl.ds(n * sources, sources)
                out_ref[blocks, 0:32, :] = new.astype(BF16).reshape(sources, 32, 128)
            return (
                ua + fold(u * plain),
                us + fold(u_on * plain),
                ga + fold(g * plain),
                gs + fold(g_on * plain),
            )

        sum_ua, sum_us, ga, gs = lax.fori_loop(
            0, ROWS // CHUNK, step, (sum_ua, sum_us, zero, zero)
        )
        ga, gs = over_q(ga), over_q(gs)
        sum_ref[2 + level : 3 + level, :] = cos_d * ga + sin_d * gs
        phi = phi + mix[level] * (cos_d * gs - sin_d * ga)
    sum_ref[0:1, :] = cos_a * over_q(sum_us) - sin_a * over_q(sum_ua)
    sum_ref[1:2, :] = phi
    group = lax.broadcasted_iota(jnp.int32, (4, 128), 1) // 32
    packed = jnp.zeros((4, 128), F32)
    for b in range(4):
        packed = jnp.where(group == b, sum_ref[4 * b : 4 * b + 4, :], packed)
    high = packed.astype(BF16).astype(F32)
    both = jnp.concatenate([high, packed - high], axis=0).astype(BF16)
    out_ref[:, 32:40, :] = jnp.broadcast_to(both[None], (64, 8, 128))


def backward(lengths, coef, received, mixed, keep):
    vmem = pl.BlockSpec(memory_space=pltpu.VMEM)
    return pl.pallas_call(
        backward_kernel,
        in_specs=[
            pl.BlockSpec(memory_space=pltpu.SMEM), vmem, vmem, vmem,
            pl.BlockSpec(memory_space=pltpu.HBM),
        ],
        out_specs=vmem,
        out_shape=jax.ShapeDtypeStruct((64, 40, 128), BF16),
        scratch_shapes=[
            pltpu.VMEM((LEVELS + 1, ROWS, 128), F32),
            pltpu.VMEM((ROWS + PAD, 128), jnp.int32),
            pltpu.VMEM((ROWS + PAD, 128), F32),
            pltpu.VMEM((2, ROWS + PAD, 128), F32),
            pltpu.VMEM((16, 128), F32),
            pltpu.SemaphoreType.DMA((LEVELS + 1,)),
        ],
        compiler_params=LARGE,
        cost_estimate=pl.CostEstimate(flops=10**8, bytes_accessed=2**25, transcendentals=2**18),
        name="backward",
    )(lengths, coef, received, mixed, keep)


def natural(in_ref, out_ref, order, tile):
    part = [in_ref[4 * tile + jj, 0:32, :].astype(F32) for jj in range(4)]
    rows = jnp.concatenate(swap_groups(part, 32), axis=0).astype(BF16)
    lanes = slice(128 * tile, 128 * tile + 128)
    out_ref[:, lanes] = dot(order, rows, ((1,), (0,))).astype(BF16)


def act_kernel(in_ref, act_ref):
    order = row_order(True)
    for tile in range(16):
        natural(in_ref, act_ref, order, tile)


def natural_act(received):
    vmem = pl.BlockSpec(memory_space=pltpu.VMEM)
    return pl.pallas_call(
        act_kernel,
        in_specs=[vmem],
        out_specs=vmem,
        out_shape=jax.ShapeDtypeStruct((128, 2048), BF16),
        cost_estimate=pl.CostEstimate(flops=10**8, bytes_accessed=2**20, transcendentals=0),
        compiler_params=SMALL,
        name="natural_act",
    )(received)


def grad_kernel(in_ref, grad_ref, sums_ref):
    order = row_order(True)
    for tile in range(16):
        natural(in_ref, grad_ref, order, tile)
        part = []
        for jj in range(4):
            both = in_ref[4 * tile + jj, 32:40, :].astype(F32)
            part.append(both[0:4] + both[4:8])
        for b, value in enumerate(swap_groups(part, 32)):
            sums_ref[4 * b : 4 * b + 4, 128 * tile : 128 * tile + 128] = value


def natural_grad(received):
    vmem = pl.BlockSpec(memory_space=pltpu.VMEM)
    return pl.pallas_call(
        grad_kernel,
        in_specs=[vmem],
        out_specs=[vmem] * 2,
        out_shape=[
            jax.ShapeDtypeStruct((128, 2048), BF16),
            jax.ShapeDtypeStruct((16, 2048), F32),
        ],
        cost_estimate=pl.CostEstimate(flops=10**8, bytes_accessed=2**20, transcendentals=0),
        compiler_params=SMALL,
        name="natural_grad",
    )(received)


def send_kernel(place_ref, in_ref, *refs):
    outs, send_ref = refs[:8], refs[8]
    x, c = place_ref[0], place_ref[1]
    for half in range(2):
        for core in range(2):
            other = jnp.where(c == core, 0, 4)
            for chunk in range(2):
                part = []
                for y in (2 * half, 2 * half + 1):
                    for z in range(8):
                        source = 8 * z + 2 * y + core
                        part.append(in_ref[source, 16 * chunk : 16 * chunk + 16, :].astype(F32))
                for at, value in enumerate(swap_groups(part, 8)):
                    q, to = at // 4, at % 4
                    row = 32 * q + 16 * chunk
                    slot = other + lax.rem(to - x + 4, 4)
                    send_ref[slot, row : row + 16, 128 * half : 128 * half + 128] = value.astype(BF16)
    for slot in range(8):
        outs[slot][...] = send_ref[slot]


def to_send(place, received):
    vmem = pl.BlockSpec(memory_space=pltpu.VMEM)
    return pl.pallas_call(
        send_kernel,
        in_specs=[pl.BlockSpec(memory_space=pltpu.SMEM), vmem],
        out_specs=[vmem] * 8,
        out_shape=[jax.ShapeDtypeStruct((128, 256), BF16)] * 8,
        scratch_shapes=[pltpu.VMEM((8, 128, 256), BF16)],
        cost_estimate=pl.CostEstimate(flops=10**8, bytes_accessed=2**20, transcendentals=0),
        compiler_params=SMALL,
        name="to_send",
    )(place, received)


def outer_kernel(place_ref, *refs):
    acts, cots, outs, act_ref = refs[:8], refs[8:16], refs[16:20], refs[20]

    @pl.when(pl.program_id(0) == 0)
    def _():
        order = row_order(False)
        for at in range(8):
            act = dot(acts[at][...], order, ((0,), (0,))).astype(BF16)
            for y in range(4):
                slot = lax.rem(y - place_ref[2] + 4, 4)
                act_ref[slot, :, 128 * at : 128 * at + 128] = act[64 * y : 64 * y + 64]

    together = jnp.concatenate([ref[...] for ref in cots], axis=0)
    total = dot(act_ref[...].reshape(256, 1024), together, ((1,), (0,))).astype(BF16)
    for slot in range(4):
        outs[slot][...] = total[64 * slot : 64 * slot + 64]


def outer(place, acts, cots):
    width = 512
    whole = pl.BlockSpec((128, 256), lambda n: (0, 0))
    part = pl.BlockSpec((128, width), lambda n: (0, n))
    return pl.pallas_call(
        outer_kernel,
        grid=(2048 // width,),
        in_specs=[pl.BlockSpec(memory_space=pltpu.SMEM)] + [whole] * 8 + [part] * 8,
        out_specs=[pl.BlockSpec((64, width), lambda n: (0, n))] * 4,
        out_shape=[jax.ShapeDtypeStruct((64, 2048), BF16)] * 4,
        scratch_shapes=[pltpu.VMEM((4, 64, 1024), BF16)],
        cost_estimate=pl.CostEstimate(flops=2**30, bytes_accessed=2**23, transcendentals=0),
        compiler_params=SMALL,
        name="outer",
    )(place, *acts, *cots)


def add_kernel(b0, b1, b2, b3, out_ref):
    total = (b0[...].astype(F32) + b1[...].astype(F32)) + (b2[...].astype(F32) + b3[...].astype(F32))
    out_ref[...] = total.astype(BF16)


def add_four(blocks):
    vmem = pl.BlockSpec(memory_space=pltpu.VMEM)
    return pl.pallas_call(
        add_kernel,
        in_specs=[vmem] * 4,
        out_specs=vmem,
        out_shape=jax.ShapeDtypeStruct((64, 2048), BF16),
        cost_estimate=pl.CostEstimate(flops=2**20, bytes_accessed=2**20, transcendentals=0),
        compiler_params=SMALL,
        name="add_four",
    )(*blocks)


def gather_kernel(in_ref, sums_ref, out_ref, *, factor):
    out_ref[0:8, :] = (jnp.sum(in_ref[...].astype(F32), axis=0) * factor).astype(BF16)
    out_ref[8:24, :] = (sums_ref[...] * factor).astype(BF16)


def gather(received, sums, factor):
    vmem = pl.BlockSpec(memory_space=pltpu.VMEM)
    return pl.pallas_call(
        functools.partial(gather_kernel, factor=factor),
        in_specs=[vmem, vmem],
        out_specs=vmem,
        out_shape=jax.ShapeDtypeStruct((24, 2048), BF16),
        cost_estimate=pl.CostEstimate(flops=2**20, bytes_accessed=2**20, transcendentals=0),
        compiler_params=SMALL,
        name="gather",
    )(received, sums)


def assemble_kernel(place_ref, b0, b1, b2, b3, weight_ref, angle_ref, mix_ref, sums_ref):
    x = place_ref[0]
    for step, ref in enumerate((b0, b1, b2, b3)):
        source = lax.rem(x - step + 4, 4)
        block = ref[...].astype(F32)
        weight_ref[pl.ds(pl.multiple_of(8 * source, 8), 8), :] = block[0:8]
        sums_ref[source] = block[8:24]
    total = (sums_ref[0] + sums_ref[1]) + (sums_ref[2] + sums_ref[3])
    angle_ref[...] = total[0:2]
    mix_ref[...] = total[2:16]


def assemble(place, blocks):
    vmem = pl.BlockSpec(memory_space=pltpu.VMEM)
    return pl.pallas_call(
        assemble_kernel,
        in_specs=[pl.BlockSpec(memory_space=pltpu.SMEM)] + [vmem] * 4,
        out_specs=[vmem] * 3,
        out_shape=[
            jax.ShapeDtypeStruct((32, 2048), F32),
            jax.ShapeDtypeStruct((2, 2048), F32),
            jax.ShapeDtypeStruct((14, 2048), F32),
        ],
        scratch_shapes=[pltpu.VMEM((4, 16, 2048), F32)],
        compiler_params=SMALL,
        name="assemble",
    )(place, *blocks)


def along(block, axis, step):
    return lax.ppermute(block, axis, [(i, (i + step) % 4) for i in range(4)])


def around(block, step, other):
    route = [(2 * i + c, 2 * ((i + step) % 4) + (c ^ other)) for i in range(4) for c in range(2)]
    return lax.ppermute(block, ("x", "c"), route)


def body(inputs, cotangent, lengths, angles, mix, weight):
    x, cot = inputs[0], cotangent[0]
    seq = ("z", "y", "c")
    place = jnp.stack([lax.axis_index(name) for name in ("x", "c", "y")]).astype(jnp.int32)
    factor = float(4 * 8192) ** (-0.5)

    def exchange(block, axes):
        return lax.all_to_all(block, axes, split_axis=0, concat_axis=0, tiled=True)

    got = exchange(pack(x, cot, weight), seq)
    cots = [cot] + [along(cot, "x", step) for step in (1, 2, 3)]

    coef = lax.dynamic_slice_in_dim(
        jnp.concatenate([angles, mix], axis=0), 32 * lax.axis_index(seq), 32, axis=1
    )
    coef = jnp.tile(coef, (1, 4))

    got, cots = lax.optimization_barrier((got, cots))
    cots = cots + [around(block, 0, 1) for block in cots]
    act, mixed, keep = forward(lengths, coef, got)
    got_act = exchange(act, seq)
    done = backward(lengths, coef, got, mixed, keep)
    done, cots = lax.optimization_barrier((done, cots))
    got_done = exchange(done, seq)

    sends = to_send(place, got_act)
    acts = [
        sends[at] if at == 0 else around(sends[at], at % 4, at // 4) for at in range(8)
    ]
    parts = outer(place, acts, cots)
    part = add_four([parts[0]] + [along(parts[step], "y", step) for step in (1, 2, 3)])
    pieces = exchange(part.reshape(8, 8, 2048), "z")
    output = jnp.dot(natural_act(got_act), weight, preferred_element_type=F32).astype(BF16)
    input_grad, sums = natural_grad(got_done)
    block = gather(pieces, sums, factor)
    weight_grad, angle_grad, mix_grad = assemble(
        place, [block] + [along(block, "x", step) for step in (1, 2, 3)]
    )
    return output[None], input_grad[None], weight_grad, angle_grad, mix_grad


def solution(mesh):
    grid = Mesh(mesh.devices.reshape(4, 8, 4, 2), ("x", "z", "y", "c"))
    seq = ("z", "y", "c")
    split = P("x", seq, None)
    in_specs = (split, split, P("x", None), P(), P(), P())
    out_specs = (split, split, P(seq, None), P(), P())
    return jax.shard_map(body, mesh=grid, in_specs=in_specs, out_specs=out_specs, check_vma=False)
```

```python
import functools
import math

import jax
import jax.numpy as jnp
from jax import lax
from jax.experimental import pallas as pl
from jax.experimental.pallas import tpu as pltpu
from jax.sharding import Mesh
from jax.sharding import PartitionSpec as P


F32 = jnp.float32
BF16 = jnp.bfloat16
ROWS = 2048
PAD = 1024
LEVELS = 13
CHUNK = 512
GELU_K = math.sqrt(2.0 / math.pi)
LARGE = pltpu.CompilerParams(vmem_limit_bytes=52 << 20)
SMALL = pltpu.CompilerParams(vmem_limit_bytes=12 << 20)


def here(axis):
    return lax.axis_index(axis)


def swap_groups(tiles, width):
    count = len(tiles)
    lane = lax.broadcasted_iota(jnp.int32, tiles[0].shape, 1)
    bit = 1
    while bit < count:
        high = (lane // width) & bit != 0
        new = list(tiles)
        for t in range(count):
            if t & bit == 0:
                a, b = tiles[t], tiles[t | bit]
                new[t] = jnp.where(high, pltpu.roll(b, bit * width, 1), a)
                new[t | bit] = jnp.where(high, b, pltpu.roll(a, 128 - bit * width, 1))
        tiles = new
        bit *= 2
    return tiles


def row_order(inverse):
    i = lax.broadcasted_iota(jnp.int32, (128, 128), 0)
    k = lax.broadcasted_iota(jnp.int32, (128, 128), 1)
    if inverse:
        i, k = k, i
    return (k == 4 * (i % 32) + i // 32).astype(F32).astype(BF16)


def dot(a, b, dims):
    return lax.dot_general(a, b, (dims, ((), ())), preferred_element_type=F32)


def pack_block(block, order, out_ref, tile0, at):
    ordered = dot(order, block, ((1,), (0,)))
    for tile in range(block.shape[1] // 128):
        part = [ordered[32 * q : 32 * q + 32, 128 * tile : 128 * tile + 128] for q in range(4)]
        for jj, value in enumerate(swap_groups(part, 32)):
            out_ref[4 * (tile0 + tile) + jj, at : at + 32, :] = value.astype(BF16)


def pack_kernel(x_ref, cot_ref, w_ref, out_ref, held_ref, sems):
    copies = [
        pltpu.make_async_copy(w_ref.at[pl.ds(256 * n, 256)], held_ref.at[n], sems.at[n])
        for n in range(8)
    ]
    for copy in copies:
        copy.start()
    order = row_order(False)
    pack_block(x_ref[...], order, out_ref, 0, 0)
    for n, copy in enumerate(copies):
        copy.wait()
        act_grad = dot(cot_ref[...], held_ref[n], ((1,), (1,))).astype(BF16)
        pack_block(act_grad, order, out_ref, 2 * n, 32)


def pack(x, cot, weight):
    vmem = pl.BlockSpec(memory_space=pltpu.VMEM)
    return pl.pallas_call(
        pack_kernel,
        in_specs=[vmem, vmem, pl.BlockSpec(memory_space=pltpu.HBM)],
        out_specs=vmem,
        out_shape=jax.ShapeDtypeStruct((64, 64, 128), BF16),
        scratch_shapes=[pltpu.VMEM((8, 256, 2048), BF16), pltpu.SemaphoreType.DMA((8,))],
        cost_estimate=pl.CostEstimate(flops=2**30, bytes_accessed=2**23, transcendentals=0),
        name="pack",
    )(x, cot, weight)


def filters(coef_ref):
    cos_a, sin_a = jnp.cos(coef_ref[0:1, :]), jnp.sin(coef_ref[0:1, :])
    cos_d, sin_d = jnp.cos(coef_ref[1:2, :]), jnp.sin(coef_ref[1:2, :])
    mix = [coef_ref[2 + level : 3 + level, :] for level in range(LEVELS + 1)]
    return cos_a, sin_a, cos_d, sin_d, mix


def positions(len_ref, r0):
    row = lax.broadcasted_iota(jnp.int32, (CHUNK, 128), 0)
    lane = lax.broadcasted_iota(jnp.int32, (CHUNK, 128), 1)
    time = 4 * (r0 + row) + lane // 32
    start = jnp.zeros((CHUNK, 128), jnp.int32)
    end = jnp.int32(0)
    for s in range(4):
        length = len_ref[0, s]
        end = end + length
        start = start + jnp.where(end <= time, length, 0)
    return time - start


def forward_kernel(len_ref, coef_ref, in_ref, act_ref, keep_ref, a_ref, pos_ref, mixed_ref, sems):
    lane = lax.broadcasted_iota(jnp.int32, (CHUNK, 128), 1)
    cos_a, sin_a, cos_d, sin_d, mix = filters(coef_ref)
    sources = CHUNK // 32

    def start_up(n, carry):
        r0 = pl.multiple_of(n * CHUNK, CHUNK)
        pos_ref[pl.ds(r0, CHUNK), :] = positions(len_ref, r0)
        got = in_ref[pl.ds(n * sources, sources), 0:32, :].astype(F32)
        a_ref[0, pl.ds(PAD + r0, CHUNK), :] = got.reshape(CHUNK, 128)
        return carry

    def save(level):
        return pltpu.make_async_copy(
            a_ref.at[level, pl.ds(PAD, ROWS)], keep_ref.at[level], sems.at[level]
        )

    lax.fori_loop(0, ROWS // CHUNK, start_up, 0)
    save(0).start()

    def behind(level, r0):
        dist = 2**level
        if dist >= 4:
            moved = a_ref[level, pl.ds(PAD + r0 - dist // 4, CHUNK), :]
        else:
            here = a_ref[level, pl.ds(PAD + r0, CHUNK), :]
            before = a_ref[level, pl.ds(PAD + r0 - 1, CHUNK), :]
            moved = pltpu.roll(jnp.where(lane >= 128 - 32 * dist, before, here), 32 * dist, 1)
        return jnp.where(pos_ref[pl.ds(r0, CHUNK), :] >= dist, moved, 0.0)

    for level in range(LEVELS):
        to_mix = mix[level] * cos_d
        to_mix_s = mix[level] * sin_d

        def step(n, carry, level=level, to_mix=to_mix, to_mix_s=to_mix_s):
            r0 = pl.multiple_of(n * CHUNK, CHUNK)
            rows = pl.ds(r0, CHUNK)
            plain = a_ref[level, pl.ds(PAD + r0, CHUNK), :]
            shifted = behind(level, r0)
            term = to_mix * plain + to_mix_s * shifted
            mixed = term if level == 0 else mixed_ref[rows, :] + term
            above = cos_a * plain + sin_a * shifted
            a_ref[level + 1, pl.ds(PAD + r0, CHUNK), :] = above
            if level == LEVELS - 1:
                mixed = mixed + mix[LEVELS] * above
                th = jnp.tanh(GELU_K * (mixed + 0.044715 * (mixed * mixed * mixed)))
                half = 0.5 * (1.0 + th)
                tail = 0.5 * mixed * (1.0 - th * th)
                slope = half + tail * (GELU_K * (1.0 + 3 * 0.044715 * (mixed * mixed)))
                blocks = pl.ds(n * sources, sources)
                act_ref[blocks] = (mixed * half).astype(BF16).reshape(sources, 32, 128)
                act_grad = in_ref[blocks, 32:64, :].astype(F32).reshape(CHUNK, 128)
                mixed = (slope * act_grad).astype(BF16).astype(F32)
            mixed_ref[rows, :] = mixed
            return carry

        lax.fori_loop(0, ROWS // CHUNK, step, 0)
        save(level + 1).start()
    last = pltpu.make_async_copy(mixed_ref, keep_ref.at[LEVELS + 1], sems.at[LEVELS + 1])
    last.start()
    for level in range(LEVELS + 1):
        save(level).wait()
    last.wait()


def forward(lengths, coef, received):
    vmem = pl.BlockSpec(memory_space=pltpu.VMEM)
    return pl.pallas_call(
        forward_kernel,
        in_specs=[pl.BlockSpec(memory_space=pltpu.SMEM), vmem, vmem],
        out_specs=[vmem, pl.BlockSpec(memory_space=pltpu.HBM)],
        out_shape=[
            jax.ShapeDtypeStruct((64, 32, 128), BF16),
            jax.ShapeDtypeStruct((LEVELS + 2, ROWS, 128), F32),
        ],
        scratch_shapes=[
            pltpu.VMEM((LEVELS + 1, PAD + ROWS, 128), F32),
            pltpu.VMEM((ROWS, 128), jnp.int32),
            pltpu.VMEM((ROWS, 128), F32),
            pltpu.SemaphoreType.DMA((LEVELS + 2,)),
        ],
        compiler_params=LARGE,
        cost_estimate=pl.CostEstimate(flops=10**8, bytes_accessed=2**25, transcendentals=2**18),
        name="forward",
    )(lengths, coef, received)


def backward_kernel(len_ref, coef_ref, keep_ref, out_ref, a_ref, pos_ref, g_ref, u_ref, sum_ref, sems):
    lane = lax.broadcasted_iota(jnp.int32, (CHUNK, 128), 1)
    cos_a, sin_a, cos_d, sin_d, mix = filters(coef_ref)
    sources = CHUNK // 32

    def load(level):
        return pltpu.make_async_copy(keep_ref.at[level], a_ref.at[level], sems.at[level])

    first = pltpu.make_async_copy(
        keep_ref.at[LEVELS + 1], g_ref.at[pl.ds(0, ROWS)], sems.at[LEVELS + 1]
    )
    first.start()
    for level in reversed(range(LEVELS + 1)):
        load(level).start()

    def fold(value):
        return jnp.sum(value.reshape(CHUNK // 8, 8, 128), axis=0)

    def over_q(value):
        row = jnp.sum(value, axis=0, keepdims=True)
        row = row + pltpu.roll(row, 32, 1)
        return row + pltpu.roll(row, 64, 1)

    zero = jnp.zeros((8, 128), F32)
    first.wait()
    load(LEVELS).wait()

    def start_up(n, carry):
        r0 = pl.multiple_of(n * CHUNK, CHUNK)
        rows = pl.ds(r0, CHUNK)
        pos_ref[rows, :] = positions(len_ref, r0)
        g = g_ref[rows, :]
        u_ref[1, rows, :] = mix[LEVELS] * g
        return carry + fold(g * a_ref[LEVELS, rows, :])

    sum_ref[15:16, :] = over_q(lax.fori_loop(0, ROWS // CHUNK, start_up, zero))
    pos_ref[pl.ds(ROWS, PAD), :] = jnp.full((PAD, 128), -1, jnp.int32)

    sum_ua, sum_us = zero, zero
    phi = jnp.zeros((1, 128), F32)
    for level in reversed(range(LEVELS)):
        dist = 2**level
        source, target = (1, 0) if level % 2 == 0 else (0, 1)
        from_g = mix[level] * cos_d
        from_g_s = mix[level] * sin_d
        load(level).wait()

        def step(n, carry, level=level, dist=dist, source=source, target=target, from_g=from_g, from_g_s=from_g_s):
            ua, us, ga, gs = carry
            r0 = pl.multiple_of(n * CHUNK, CHUNK)
            rows = pl.ds(r0, CHUNK)
            u, g = u_ref[source, rows, :], g_ref[rows, :]
            if dist >= 4:
                later = pl.ds(r0 + dist // 4, CHUNK)
                u_on, g_on, pos = u_ref[source, later, :], g_ref[later, :], pos_ref[later, :]
            else:
                later = pl.ds(r0 + 1, CHUNK)

                def ahead(here, there):
                    return pltpu.roll(jnp.where(lane < 32 * dist, there, here), 128 - 32 * dist, 1)

                u_on = ahead(u, u_ref[source, later, :])
                g_on = ahead(g, g_ref[later, :])
                pos = ahead(pos_ref[rows, :], pos_ref[later, :])
            keep = pos >= dist
            u_on = jnp.where(keep, u_on, 0.0)
            g_on = jnp.where(keep, g_on, 0.0)
            new = (cos_a * u + from_g * g) + (sin_a * u_on + from_g_s * g_on)
            plain = a_ref[level, rows, :]
            if level > 0:
                u_ref[target, rows, :] = new
            else:
                blocks = pl.ds(n * sources, sources)
                out_ref[blocks, 0:32, :] = new.astype(BF16).reshape(sources, 32, 128)
            return (
                ua + fold(u * plain),
                us + fold(u_on * plain),
                ga + fold(g * plain),
                gs + fold(g_on * plain),
            )

        sum_ua, sum_us, ga, gs = lax.fori_loop(
            0, ROWS // CHUNK, step, (sum_ua, sum_us, zero, zero)
        )
        ga, gs = over_q(ga), over_q(gs)
        sum_ref[2 + level : 3 + level, :] = cos_d * ga + sin_d * gs
        phi = phi + mix[level] * (cos_d * gs - sin_d * ga)
    sum_ref[0:1, :] = cos_a * over_q(sum_us) - sin_a * over_q(sum_ua)
    sum_ref[1:2, :] = phi
    group = lax.broadcasted_iota(jnp.int32, (4, 128), 1) // 32
    packed = jnp.zeros((4, 128), F32)
    for b in range(4):
        packed = jnp.where(group == b, sum_ref[4 * b : 4 * b + 4, :], packed)
    high = packed.astype(BF16).astype(F32)
    both = jnp.concatenate([high, packed - high], axis=0).astype(BF16)
    out_ref[:, 32:40, :] = jnp.broadcast_to(both[None], (64, 8, 128))


def backward(lengths, coef, keep):
    vmem = pl.BlockSpec(memory_space=pltpu.VMEM)
    return pl.pallas_call(
        backward_kernel,
        in_specs=[
            pl.BlockSpec(memory_space=pltpu.SMEM), vmem, pl.BlockSpec(memory_space=pltpu.HBM),
        ],
        out_specs=vmem,
        out_shape=jax.ShapeDtypeStruct((64, 40, 128), BF16),
        scratch_shapes=[
            pltpu.VMEM((LEVELS + 1, ROWS, 128), F32),
            pltpu.VMEM((ROWS + PAD, 128), jnp.int32),
            pltpu.VMEM((ROWS + PAD, 128), F32),
            pltpu.VMEM((2, ROWS + PAD, 128), F32),
            pltpu.VMEM((16, 128), F32),
            pltpu.SemaphoreType.DMA((LEVELS + 2,)),
        ],
        compiler_params=LARGE,
        cost_estimate=pl.CostEstimate(flops=10**8, bytes_accessed=2**25, transcendentals=2**18),
        name="backward",
    )(lengths, coef, keep)


def natural(in_ref, out_ref, order, tile):
    part = [in_ref[4 * tile + jj, 0:32, :].astype(F32) for jj in range(4)]
    rows = jnp.concatenate(swap_groups(part, 32), axis=0).astype(BF16)
    lanes = slice(128 * tile, 128 * tile + 128)
    out_ref[:, lanes] = dot(order, rows, ((1,), (0,))).astype(BF16)


def act_kernel(in_ref, act_ref):
    order = row_order(True)
    for tile in range(16):
        natural(in_ref, act_ref, order, tile)


def natural_act(received):
    vmem = pl.BlockSpec(memory_space=pltpu.VMEM)
    return pl.pallas_call(
        act_kernel,
        in_specs=[vmem],
        out_specs=vmem,
        out_shape=jax.ShapeDtypeStruct((128, 2048), BF16),
        cost_estimate=pl.CostEstimate(flops=10**8, bytes_accessed=2**20, transcendentals=0),
        compiler_params=SMALL,
        name="natural_act",
    )(received)


def grad_kernel(in_ref, grad_ref, sums_ref):
    order = row_order(True)
    for tile in range(16):
        natural(in_ref, grad_ref, order, tile)
        part = []
        for jj in range(4):
            both = in_ref[4 * tile + jj, 32:40, :].astype(F32)
            part.append(both[0:4] + both[4:8])
        for b, value in enumerate(swap_groups(part, 32)):
            sums_ref[4 * b : 4 * b + 4, 128 * tile : 128 * tile + 128] = value


def natural_grad(received):
    vmem = pl.BlockSpec(memory_space=pltpu.VMEM)
    return pl.pallas_call(
        grad_kernel,
        in_specs=[vmem],
        out_specs=[vmem] * 2,
        out_shape=[
            jax.ShapeDtypeStruct((128, 2048), BF16),
            jax.ShapeDtypeStruct((16, 2048), F32),
        ],
        cost_estimate=pl.CostEstimate(flops=10**8, bytes_accessed=2**20, transcendentals=0),
        compiler_params=SMALL,
        name="natural_grad",
    )(received)


def send_kernel(in_ref, *refs):
    outs, send_ref = refs[:4], refs[4]
    x, c = here("x"), here("c")
    for half in range(2):
        for core in range(2):
            other = jnp.where(c == core, 0, 1)
            for chunk in range(2):
                part = []
                for y in (2 * half, 2 * half + 1):
                    for z in range(8):
                        source = 8 * z + 2 * y + core
                        part.append(in_ref[source, 16 * chunk : 16 * chunk + 16, :].astype(F32))
                for at, value in enumerate(swap_groups(part, 8)):
                    q, to = at // 4, at % 4
                    row = 32 * q + 16 * chunk
                    slot = 2 * lax.rem(to - x + 4, 4) + other
                    send_ref[slot, row : row + 16, 128 * half : 128 * half + 128] = value.astype(BF16)
    for step in range(4):
        outs[step][...] = send_ref[2 * step : 2 * step + 2]


def to_send(received):
    vmem = pl.BlockSpec(memory_space=pltpu.VMEM)
    return pl.pallas_call(
        send_kernel,
        in_specs=[vmem],
        out_specs=[vmem] * 4,
        out_shape=[jax.ShapeDtypeStruct((2, 128, 256), BF16)] * 4,
        scratch_shapes=[pltpu.VMEM((8, 128, 256), BF16)],
        compiler_params=SMALL,
        cost_estimate=pl.CostEstimate(flops=10**8, bytes_accessed=2**20, transcendentals=0),
        name="to_send",
    )(received)


def outer_kernel(*refs):
    acts, cots, outs, act_ref = refs[:8], refs[8:16], refs[16:20], refs[20]

    @pl.when(pl.program_id(0) == 0)
    def _():
        order = row_order(False)
        for at in range(8):
            act = dot(acts[at][0], order, ((0,), (0,))).astype(BF16)
            for y in range(4):
                slot = lax.rem(y - here("y") + 4, 4)
                act_ref[slot, :, 128 * at : 128 * at + 128] = act[64 * y : 64 * y + 64]

    together = jnp.concatenate([ref[...] for ref in cots], axis=0)
    total = dot(act_ref[...].reshape(256, 1024), together, ((1,), (0,))).astype(BF16)
    for slot in range(4):
        outs[slot][...] = total[64 * slot : 64 * slot + 64]


def outer(near, far, cots):
    width = 1024
    own = pl.BlockSpec((1, 128, 256), lambda n: (0, 0, 0))
    other = pl.BlockSpec((1, 128, 256), lambda n: (1, 0, 0))
    part = pl.BlockSpec((128, width), lambda n: (0, n))
    return pl.pallas_call(
        outer_kernel,
        grid=(2048 // width,),
        in_specs=[own] * 4 + [other] * 4 + [part] * 8,
        out_specs=[pl.BlockSpec((64, width), lambda n: (0, n))] * 4,
        out_shape=[jax.ShapeDtypeStruct((64, 2048), BF16)] * 4,
        scratch_shapes=[pltpu.VMEM((4, 64, 1024), BF16)],
        cost_estimate=pl.CostEstimate(flops=2**30, bytes_accessed=2**23, transcendentals=0),
        name="outer",
    )(*near, *far, *cots)


def add_kernel(b0, b1, b2, b3, *refs):
    outs, total_ref = refs[:8], refs[8]
    total_ref[...] = (b0[...].astype(F32) + b1[...].astype(F32)) + (b2[...].astype(F32) + b3[...].astype(F32))
    for step in range(8):
        row = pl.multiple_of(8 * lax.rem(here("z") + step, 8), 8)
        outs[step][...] = total_ref[pl.ds(row, 8), :].astype(BF16)


def add_four(blocks):
    vmem = pl.BlockSpec(memory_space=pltpu.VMEM)
    return pl.pallas_call(
        add_kernel,
        in_specs=[vmem] * 4,
        out_specs=[vmem] * 8,
        out_shape=[jax.ShapeDtypeStruct((8, 2048), BF16)] * 8,
        scratch_shapes=[pltpu.VMEM((64, 2048), F32)],
        compiler_params=SMALL,
        cost_estimate=pl.CostEstimate(flops=2**20, bytes_accessed=2**20, transcendentals=0),
        name="add_four",
    )(*blocks)


def gather_kernel(*refs, factor):
    blocks, sums_ref, out_ref = refs[:8], refs[8], refs[9]
    total = blocks[0][...].astype(F32)
    for ref in blocks[1:]:
        total = total + ref[...].astype(F32)
    out_ref[0:8, :] = (total * factor).astype(BF16)
    out_ref[8:24, :] = (sums_ref[...] * factor).astype(BF16)


def gather(blocks, sums, factor):
    vmem = pl.BlockSpec(memory_space=pltpu.VMEM)
    return pl.pallas_call(
        functools.partial(gather_kernel, factor=factor),
        in_specs=[vmem] * 9,
        out_specs=vmem,
        out_shape=jax.ShapeDtypeStruct((24, 2048), BF16),
        compiler_params=SMALL,
        cost_estimate=pl.CostEstimate(flops=2**20, bytes_accessed=2**20, transcendentals=0),
        name="gather",
    )(*blocks, sums)


def assemble_kernel(b0, b1, b2, b3, weight_ref, angle_ref, mix_ref, sums_ref):
    x = here("x")
    for step, ref in enumerate((b0, b1, b2, b3)):
        source = lax.rem(x - step + 4, 4)
        block = ref[...].astype(F32)
        weight_ref[pl.ds(pl.multiple_of(8 * source, 8), 8), :] = block[0:8]
        sums_ref[source] = block[8:24]
    total = (sums_ref[0] + sums_ref[1]) + (sums_ref[2] + sums_ref[3])
    angle_ref[...] = total[0:2]
    mix_ref[...] = total[2:16]


def assemble(blocks):
    vmem = pl.BlockSpec(memory_space=pltpu.VMEM)
    return pl.pallas_call(
        assemble_kernel,
        in_specs=[vmem] * 4,
        out_specs=[vmem] * 3,
        out_shape=[
            jax.ShapeDtypeStruct((32, 2048), F32),
            jax.ShapeDtypeStruct((2, 2048), F32),
            jax.ShapeDtypeStruct((14, 2048), F32),
        ],
        scratch_shapes=[pltpu.VMEM((4, 16, 2048), F32)],
        compiler_params=SMALL,
        name="assemble",
    )(*blocks)


def along(block, axis, step):
    size = lax.axis_size(axis)
    return lax.ppermute(block, axis, [(i, (i + step) % size) for i in range(size)])


def other_core(block):
    return lax.ppermute(block, "c", [(0, 1), (1, 0)])


def body(inputs, cotangent, lengths, angles, mix, weight):
    x, cot = inputs[0], cotangent[0]
    seq = ("z", "y", "c")
    factor = float(4 * 8192) ** (-0.5)

    def exchange(block):
        return lax.all_to_all(block, seq, split_axis=0, concat_axis=0, tiled=True)

    got = exchange(pack(x, cot, weight))
    cots = [cot] + [along(cot, "x", step) for step in (1, 2, 3)]

    coef = lax.dynamic_slice_in_dim(
        jnp.concatenate([angles, mix], axis=0), 32 * lax.axis_index(seq), 32, axis=1
    )
    coef = jnp.tile(coef, (1, 4))

    got, cots = lax.optimization_barrier((got, cots))
    cots = cots + [other_core(block) for block in cots]
    act, keep = forward(lengths, coef, got)
    got_act = exchange(act)
    done = backward(lengths, coef, keep)
    done, cots, got_act = lax.optimization_barrier((done, cots, got_act))

    sends = to_send(got_act)
    near = [sends[0]] + [along(sends[step], "x", step) for step in (1, 2, 3)]
    far = [other_core(block) for block in near]
    parts = outer(near, far, cots)
    output = jnp.dot(natural_act(got_act), weight, preferred_element_type=F32).astype(BF16)
    parts = [parts[0]] + [along(parts[step], "y", step) for step in (1, 2, 3)]
    got_done = exchange(done)
    parts = add_four(parts)
    parts = [parts[0]] + [along(parts[step], "z", step) for step in range(1, 8)]
    input_grad, sums = natural_grad(got_done)
    block = gather(parts, sums, factor)
    weight_grad, angle_grad, mix_grad = assemble(
        [block] + [along(block, "x", step) for step in (1, 2, 3)]
    )
    return output[None], input_grad[None], weight_grad, angle_grad, mix_grad


def solution(mesh):
    grid = Mesh(mesh.devices.reshape(4, 8, 4, 2), ("x", "z", "y", "c"))
    seq = ("z", "y", "c")
    split = P("x", seq, None)
    in_specs = (split, split, P("x", None), P(), P(), P())
    out_specs = (split, split, P(seq, None), P(), P())
    return jax.shard_map(body, mesh=grid, in_specs=in_specs, out_specs=out_specs, check_vma=False)
```

```python
import functools
import math

import jax
import jax.numpy as jnp
from jax import lax
from jax.experimental import pallas as pl
from jax.experimental.pallas import tpu as pltpu
from jax.sharding import Mesh
from jax.sharding import PartitionSpec as P


F32 = jnp.float32
BF16 = jnp.bfloat16
ROWS = 2048
PAD = 1024
LEVELS = 13
CHUNK = 512
GELU_K = math.sqrt(2.0 / math.pi)
LARGE = pltpu.CompilerParams(vmem_limit_bytes=52 << 20)
SMALL = pltpu.CompilerParams(vmem_limit_bytes=12 << 20)


def here(axis):
    return lax.axis_index(axis)


def swap_groups(tiles, width):
    count = len(tiles)
    lane = lax.broadcasted_iota(jnp.int32, tiles[0].shape, 1)
    bit = 1
    while bit < count:
        high = (lane // width) & bit != 0
        new = list(tiles)
        for t in range(count):
            if t & bit == 0:
                a, b = tiles[t], tiles[t | bit]
                new[t] = jnp.where(high, pltpu.roll(b, bit * width, 1), a)
                new[t | bit] = jnp.where(high, b, pltpu.roll(a, 128 - bit * width, 1))
        tiles = new
        bit *= 2
    return tiles


def row_order(inverse):
    i = lax.broadcasted_iota(jnp.int32, (128, 128), 0)
    k = lax.broadcasted_iota(jnp.int32, (128, 128), 1)
    if inverse:
        i, k = k, i
    return (k == 4 * (i % 32) + i // 32).astype(F32).astype(BF16)


def dot(a, b, dims):
    return lax.dot_general(a, b, (dims, ((), ())), preferred_element_type=F32)


def pack_kernel(x_ref, grad_ref, out_ref):
    order = row_order(False)
    for at, block in ((0, x_ref), (32, grad_ref)):
        ordered = dot(order, block[...], ((1,), (0,)))
        for tile in range(block.shape[1] // 128):
            part = [ordered[32 * q : 32 * q + 32, 128 * tile : 128 * tile + 128] for q in range(4)]
            for jj, value in enumerate(swap_groups(part, 32)):
                out_ref[4 * tile + jj, at : at + 32, :] = value.astype(BF16)


def pack(x, act_grad):
    width = 1024
    part = pl.BlockSpec((128, width), lambda n: (0, n))
    return pl.pallas_call(
        pack_kernel,
        grid=(2048 // width,),
        in_specs=[part, part],
        out_specs=pl.BlockSpec((width // 32, 64, 128), lambda n: (n, 0, 0)),
        out_shape=jax.ShapeDtypeStruct((64, 64, 128), BF16),
        compiler_params=SMALL,
        cost_estimate=pl.CostEstimate(flops=10**8, bytes_accessed=2**21, transcendentals=0),
        name="pack",
    )(x, act_grad)


def filters(coef_ref):
    cos_a, sin_a = jnp.cos(coef_ref[0:1, :]), jnp.sin(coef_ref[0:1, :])
    cos_d, sin_d = jnp.cos(coef_ref[1:2, :]), jnp.sin(coef_ref[1:2, :])
    mix = [coef_ref[2 + level : 3 + level, :] for level in range(LEVELS + 1)]
    return cos_a, sin_a, cos_d, sin_d, mix


def positions(len_ref, r0):
    row = lax.broadcasted_iota(jnp.int32, (CHUNK, 128), 0)
    lane = lax.broadcasted_iota(jnp.int32, (CHUNK, 128), 1)
    time = 4 * (r0 + row) + lane // 32
    start = jnp.zeros((CHUNK, 128), jnp.int32)
    end = jnp.int32(0)
    for s in range(4):
        length = len_ref[0, s]
        end = end + length
        start = start + jnp.where(end <= time, length, 0)
    return time - start


def two_parts(value):
    high = value.astype(BF16).astype(F32)
    return jnp.concatenate([high, value - high], axis=0).astype(BF16)


def forward_kernel(len_ref, coef_ref, in_ref, act_ref, keep_ref, a_ref, pos_ref, mixed_ref, sems):
    lane = lax.broadcasted_iota(jnp.int32, (CHUNK, 128), 1)
    cos_a, sin_a, cos_d, sin_d, mix = filters(coef_ref)
    sources = CHUNK // 32

    def start_up(n, carry):
        r0 = pl.multiple_of(n * CHUNK, CHUNK)
        pos_ref[pl.ds(r0, CHUNK), :] = positions(len_ref, r0)
        got = in_ref[pl.ds(n * sources, sources), 0:32, :].astype(F32)
        a_ref[0, pl.ds(PAD + r0, CHUNK), :] = got.reshape(CHUNK, 128)
        return carry

    def save(level):
        return pltpu.make_async_copy(
            a_ref.at[level, pl.ds(PAD, ROWS)], keep_ref.at[level], sems.at[level]
        )

    lax.fori_loop(0, ROWS // CHUNK, start_up, 0)
    save(0).start()

    def behind(level, r0):
        dist = 2**level
        if dist >= 4:
            moved = a_ref[level, pl.ds(PAD + r0 - dist // 4, CHUNK), :]
        else:
            here = a_ref[level, pl.ds(PAD + r0, CHUNK), :]
            before = a_ref[level, pl.ds(PAD + r0 - 1, CHUNK), :]
            moved = pltpu.roll(jnp.where(lane >= 128 - 32 * dist, before, here), 32 * dist, 1)
        return jnp.where(pos_ref[pl.ds(r0, CHUNK), :] >= dist, moved, 0.0)

    for level in range(LEVELS):
        to_mix = mix[level] * cos_d
        to_mix_s = mix[level] * sin_d

        def step(n, carry, level=level, to_mix=to_mix, to_mix_s=to_mix_s):
            r0 = pl.multiple_of(n * CHUNK, CHUNK)
            rows = pl.ds(r0, CHUNK)
            plain = a_ref[level, pl.ds(PAD + r0, CHUNK), :]
            shifted = behind(level, r0)
            term = to_mix * plain + to_mix_s * shifted
            mixed = term if level == 0 else mixed_ref[rows, :] + term
            above = cos_a * plain + sin_a * shifted
            a_ref[level + 1, pl.ds(PAD + r0, CHUNK), :] = above
            if level == LEVELS - 1:
                mixed = mixed + mix[LEVELS] * above
                th = jnp.tanh(GELU_K * (mixed + 0.044715 * (mixed * mixed * mixed)))
                half = 0.5 * (1.0 + th)
                tail = 0.5 * mixed * (1.0 - th * th)
                slope = half + tail * (GELU_K * (1.0 + 3 * 0.044715 * (mixed * mixed)))
                blocks = pl.ds(n * sources, sources)
                act_ref[blocks] = (mixed * half).astype(BF16).reshape(sources, 32, 128)
                act_grad = in_ref[blocks, 32:64, :].astype(F32).reshape(CHUNK, 128)
                mixed = (slope * act_grad).astype(BF16).astype(F32)
            mixed_ref[rows, :] = mixed
            return carry

        lax.fori_loop(0, ROWS // CHUNK, step, 0)
        save(level + 1).start()
    last = pltpu.make_async_copy(mixed_ref, keep_ref.at[LEVELS + 1], sems.at[LEVELS + 1])
    last.start()
    for level in range(LEVELS + 1):
        save(level).wait()
    last.wait()


def forward(lengths, coef, received):
    vmem = pl.BlockSpec(memory_space=pltpu.VMEM)
    return pl.pallas_call(
        forward_kernel,
        in_specs=[pl.BlockSpec(memory_space=pltpu.SMEM), vmem, vmem],
        out_specs=[vmem, pl.BlockSpec(memory_space=pltpu.HBM)],
        out_shape=[
            jax.ShapeDtypeStruct((64, 32, 128), BF16),
            jax.ShapeDtypeStruct((LEVELS + 2, ROWS, 128), F32),
        ],
        scratch_shapes=[
            pltpu.VMEM((LEVELS + 1, PAD + ROWS, 128), F32),
            pltpu.VMEM((ROWS, 128), jnp.int32),
            pltpu.VMEM((ROWS, 128), F32),
            pltpu.SemaphoreType.DMA((LEVELS + 2,)),
        ],
        compiler_params=LARGE,
        cost_estimate=pl.CostEstimate(flops=10**8, bytes_accessed=2**25, transcendentals=2**18),
        name="forward",
    )(lengths, coef, received)


def backward_kernel(len_ref, coef_ref, keep_ref, out_ref, tail_ref, a_ref, pos_ref, g_ref, u_ref, sum_ref, sems):
    lane = lax.broadcasted_iota(jnp.int32, (CHUNK, 128), 1)
    cos_a, sin_a, cos_d, sin_d, mix = filters(coef_ref)
    sources = CHUNK // 32

    def load(level):
        return pltpu.make_async_copy(keep_ref.at[level], a_ref.at[level], sems.at[level])

    first = pltpu.make_async_copy(
        keep_ref.at[LEVELS + 1], g_ref.at[pl.ds(0, ROWS)], sems.at[LEVELS + 1]
    )
    first.start()
    for level in reversed(range(LEVELS + 1)):
        load(level).start()

    def fold(value):
        return jnp.sum(value.reshape(CHUNK // 8, 8, 128), axis=0)

    def over_q(value):
        row = jnp.sum(value, axis=0, keepdims=True)
        row = row + pltpu.roll(row, 32, 1)
        return row + pltpu.roll(row, 64, 1)

    zero = jnp.zeros((8, 128), F32)
    first.wait()
    load(LEVELS).wait()

    def start_up(n, carry):
        r0 = pl.multiple_of(n * CHUNK, CHUNK)
        rows = pl.ds(r0, CHUNK)
        pos_ref[rows, :] = positions(len_ref, r0)
        g = g_ref[rows, :]
        u_ref[1, rows, :] = mix[LEVELS] * g
        return carry + fold(g * a_ref[LEVELS, rows, :])

    sum_ref[15:16, :] = over_q(lax.fori_loop(0, ROWS // CHUNK, start_up, zero))
    pos_ref[pl.ds(ROWS, PAD), :] = jnp.full((PAD, 128), -1, jnp.int32)

    sum_ua, sum_us = zero, zero
    phi = jnp.zeros((1, 128), F32)
    for level in reversed(range(LEVELS)):
        dist = 2**level
        source, target = (1, 0) if level % 2 == 0 else (0, 1)
        from_g = mix[level] * cos_d
        from_g_s = mix[level] * sin_d
        load(level).wait()

        def step(n, carry, level=level, dist=dist, source=source, target=target, from_g=from_g, from_g_s=from_g_s):
            ua, us, ga, gs = carry
            r0 = pl.multiple_of(n * CHUNK, CHUNK)
            rows = pl.ds(r0, CHUNK)
            u, g = u_ref[source, rows, :], g_ref[rows, :]
            if dist >= 4:
                later = pl.ds(r0 + dist // 4, CHUNK)
                u_on, g_on, pos = u_ref[source, later, :], g_ref[later, :], pos_ref[later, :]
            else:
                later = pl.ds(r0 + 1, CHUNK)

                def ahead(here, there):
                    return pltpu.roll(jnp.where(lane < 32 * dist, there, here), 128 - 32 * dist, 1)

                u_on = ahead(u, u_ref[source, later, :])
                g_on = ahead(g, g_ref[later, :])
                pos = ahead(pos_ref[rows, :], pos_ref[later, :])
            keep = pos >= dist
            u_on = jnp.where(keep, u_on, 0.0)
            g_on = jnp.where(keep, g_on, 0.0)
            new = (cos_a * u + from_g * g) + (sin_a * u_on + from_g_s * g_on)
            plain = a_ref[level, rows, :]
            if level > 0:
                u_ref[target, rows, :] = new
            else:
                blocks = pl.ds(n * sources, sources)
                out_ref[blocks, 0:32, :] = new.astype(BF16).reshape(sources, 32, 128)
            return (
                ua + fold(u * plain),
                us + fold(u_on * plain),
                ga + fold(g * plain),
                gs + fold(g_on * plain),
            )

        sum_ua, sum_us, ga, gs = lax.fori_loop(
            0, ROWS // CHUNK, step, (sum_ua, sum_us, zero, zero)
        )
        ga, gs = over_q(ga), over_q(gs)
        sum_ref[2 + level : 3 + level, :] = cos_d * ga + sin_d * gs
        phi = phi + mix[level] * (cos_d * gs - sin_d * ga)
    sum_ref[0:1, :] = cos_a * over_q(sum_us) - sin_a * over_q(sum_ua)
    sum_ref[1:2, :] = phi
    group = lax.broadcasted_iota(jnp.int32, (4, 128), 1) // 32
    packed = jnp.zeros((4, 128), F32)
    for b in range(4):
        packed = jnp.where(group == b, sum_ref[4 * b : 4 * b + 4, :], packed)
    tail_ref[...] = two_parts(packed)


def backward(lengths, coef, keep):
    vmem = pl.BlockSpec(memory_space=pltpu.VMEM)
    return pl.pallas_call(
        backward_kernel,
        in_specs=[
            pl.BlockSpec(memory_space=pltpu.SMEM), vmem, pl.BlockSpec(memory_space=pltpu.HBM),
        ],
        out_specs=[vmem] * 2,
        out_shape=[
            jax.ShapeDtypeStruct((64, 40, 128), BF16),
            jax.ShapeDtypeStruct((8, 128), BF16),
        ],
        scratch_shapes=[
            pltpu.VMEM((LEVELS + 1, ROWS, 128), F32),
            pltpu.VMEM((ROWS + PAD, 128), jnp.int32),
            pltpu.VMEM((ROWS + PAD, 128), F32),
            pltpu.VMEM((2, ROWS + PAD, 128), F32),
            pltpu.VMEM((16, 128), F32),
            pltpu.SemaphoreType.DMA((LEVELS + 2,)),
        ],
        compiler_params=LARGE,
        cost_estimate=pl.CostEstimate(flops=10**8, bytes_accessed=2**25, transcendentals=2**18),
        name="backward",
    )(lengths, coef, keep)


def natural(in_ref, out_ref, order, tile):
    part = [in_ref[4 * tile + jj, 0:32, :].astype(F32) for jj in range(4)]
    rows = jnp.concatenate(swap_groups(part, 32), axis=0).astype(BF16)
    lanes = slice(128 * tile, 128 * tile + 128)
    out_ref[:, lanes] = dot(order, rows, ((1,), (0,))).astype(BF16)


def act_kernel(in_ref, act_ref):
    order = row_order(True)
    for tile in range(16):
        natural(in_ref, act_ref, order, tile)


def natural_act(received):
    vmem = pl.BlockSpec(memory_space=pltpu.VMEM)
    return pl.pallas_call(
        act_kernel,
        in_specs=[vmem],
        out_specs=vmem,
        out_shape=jax.ShapeDtypeStruct((128, 2048), BF16),
        cost_estimate=pl.CostEstimate(flops=10**8, bytes_accessed=2**20, transcendentals=0),
        compiler_params=SMALL,
        name="natural_act",
    )(received)


def grad_kernel(in_ref, grad_ref, angle_ref, mix_ref, sums_ref, *, factor):
    order = row_order(True)
    for tile in range(16):
        natural(in_ref, grad_ref, order, tile)
        part = []
        for jj in range(4):
            both = in_ref[4 * tile + jj, 32:40, :].astype(F32)
            part.append((both[0:4] + both[4:8]) * factor)
        for b, value in enumerate(swap_groups(part, 32)):
            sums_ref[4 * b : 4 * b + 4, 128 * tile : 128 * tile + 128] = value
    angle_ref[...] = sums_ref[0:2, :]
    mix_ref[...] = sums_ref[2:16, :]


def natural_grad(received, factor):
    vmem = pl.BlockSpec(memory_space=pltpu.VMEM)
    return pl.pallas_call(
        functools.partial(grad_kernel, factor=factor),
        in_specs=[vmem],
        out_specs=[vmem] * 3,
        out_shape=[
            jax.ShapeDtypeStruct((128, 2048), BF16),
            jax.ShapeDtypeStruct((2, 2048), F32),
            jax.ShapeDtypeStruct((14, 2048), F32),
        ],
        scratch_shapes=[pltpu.VMEM((16, 2048), F32)],
        cost_estimate=pl.CostEstimate(flops=10**8, bytes_accessed=2**20, transcendentals=0),
        compiler_params=SMALL,
        name="natural_grad",
    )(received)


def send_kernel(in_ref, tail_ref, *refs):
    outs, send_ref = refs[:8], refs[8]
    x, c = here("x"), here("c")
    for half in range(2):
        for core in range(2):
            other = jnp.where(c == core, 0, 4)
            for chunk in range(2):
                part = []
                for y in (2 * half, 2 * half + 1):
                    for z in range(8):
                        source = 8 * z + 2 * y + core
                        part.append(in_ref[source, 16 * chunk : 16 * chunk + 16, :].astype(F32))
                for at, value in enumerate(swap_groups(part, 8)):
                    q, to = at // 4, at % 4
                    row = 32 * q + 16 * chunk
                    slot = other + lax.rem(to - x + 4, 4)
                    send_ref[slot, row : row + 16, 128 * half : 128 * half + 128] = value.astype(BF16)
    for slot in range(8):
        outs[slot][0:128, :] = send_ref[slot]
        if slot < 4:
            outs[slot][128:136, 0:128] = tail_ref[...]
            outs[slot][128:136, 128:256] = tail_ref[...]


def to_send(received, tail):
    vmem = pl.BlockSpec(memory_space=pltpu.VMEM)
    return pl.pallas_call(
        send_kernel,
        in_specs=[vmem] * 2,
        out_specs=[vmem] * 8,
        out_shape=[jax.ShapeDtypeStruct((136, 256), BF16)] * 4
        + [jax.ShapeDtypeStruct((128, 256), BF16)] * 4,
        scratch_shapes=[pltpu.VMEM((8, 128, 256), BF16)],
        compiler_params=SMALL,
        cost_estimate=pl.CostEstimate(flops=10**8, bytes_accessed=2**20, transcendentals=0),
        name="to_send",
    )(received, tail)


def merge_kernel(done_ref, t0, t1, t2, t3, out_ref, slot_ref, both_ref, sem):
    x = here("x")
    for step, ref in enumerate((t0, t1, t2, t3)):
        both = ref[:, 0:128].astype(F32)
        slot_ref[lax.rem(x - step + 4, 4)] = both[0:4] + both[4:8]
    total = (slot_ref[0] + slot_ref[1]) + (slot_ref[2] + slot_ref[3])
    both_ref[...] = jnp.broadcast_to(two_parts(total)[None], (64, 8, 128))
    copy = pltpu.make_async_copy(both_ref, out_ref.at[:, pl.ds(32, 8)], sem)
    copy.start()
    copy.wait()


def merge(done, blocks):
    hbm = pl.BlockSpec(memory_space=pltpu.HBM)
    return pl.pallas_call(
        merge_kernel,
        grid=(1,),
        in_specs=[hbm] + [pl.BlockSpec((8, 256), lambda n: (16, 0))] * 4,
        out_specs=hbm,
        out_shape=jax.ShapeDtypeStruct((64, 40, 128), BF16),
        scratch_shapes=[
            pltpu.VMEM((4, 4, 128), F32),
            pltpu.VMEM((64, 8, 128), BF16),
            pltpu.SemaphoreType.DMA,
        ],
        input_output_aliases={0: 0},
        cost_estimate=pl.CostEstimate(flops=2**16, bytes_accessed=2**18, transcendentals=0),
        name="merge",
    )(done, *blocks)


def outer_kernel(*refs):
    acts, cots, outs, act_ref = refs[:8], refs[8:16], refs[16:20], refs[20]

    @pl.when(pl.program_id(0) == 0)
    def _():
        order = row_order(False)
        for at in range(8):
            act = dot(acts[at][...], order, ((0,), (0,))).astype(BF16)
            for y in range(4):
                slot = lax.rem(y - here("y") + 4, 4)
                act_ref[slot, :, 128 * at : 128 * at + 128] = act[64 * y : 64 * y + 64]

    together = jnp.concatenate([ref[...] for ref in cots], axis=0)
    total = dot(act_ref[...].reshape(256, 1024), together, ((1,), (0,))).astype(BF16)
    for slot in range(4):
        outs[slot][...] = total[64 * slot : 64 * slot + 64]


def outer(acts, cots):
    width = 1024
    whole = pl.BlockSpec((128, 256), lambda n: (0, 0))
    part = pl.BlockSpec((128, width), lambda n: (0, n))
    return pl.pallas_call(
        outer_kernel,
        grid=(2048 // width,),
        in_specs=[whole] * 8 + [part] * 8,
        out_specs=[pl.BlockSpec((64, width), lambda n: (0, n))] * 4,
        out_shape=[jax.ShapeDtypeStruct((64, 2048), BF16)] * 4,
        scratch_shapes=[pltpu.VMEM((4, 64, 1024), BF16)],
        cost_estimate=pl.CostEstimate(flops=2**30, bytes_accessed=2**23, transcendentals=0),
        name="outer",
    )(*acts, *cots)


def add_kernel(b0, b1, b2, b3, *refs):
    outs, total_ref = refs[:8], refs[8]
    total_ref[...] = (b0[...].astype(F32) + b1[...].astype(F32)) + (b2[...].astype(F32) + b3[...].astype(F32))
    for step in range(8):
        row = pl.multiple_of(8 * lax.rem(here("z") + step, 8), 8)
        outs[step][...] = total_ref[pl.ds(row, 8), :].astype(BF16)


def add_four(blocks):
    vmem = pl.BlockSpec(memory_space=pltpu.VMEM)
    return pl.pallas_call(
        add_kernel,
        in_specs=[vmem] * 4,
        out_specs=[vmem] * 8,
        out_shape=[jax.ShapeDtypeStruct((8, 2048), BF16)] * 8,
        scratch_shapes=[pltpu.VMEM((64, 2048), F32)],
        compiler_params=SMALL,
        cost_estimate=pl.CostEstimate(flops=2**20, bytes_accessed=2**20, transcendentals=0),
        name="add_four",
    )(*blocks)


def gather_kernel(*refs, factor):
    blocks, out_ref = refs[:8], refs[8]
    total = blocks[0][...].astype(F32)
    for ref in blocks[1:]:
        total = total + ref[...].astype(F32)
    out_ref[...] = (total * factor).astype(BF16)


def gather(blocks, factor):
    vmem = pl.BlockSpec(memory_space=pltpu.VMEM)
    return pl.pallas_call(
        functools.partial(gather_kernel, factor=factor),
        in_specs=[vmem] * 8,
        out_specs=vmem,
        out_shape=jax.ShapeDtypeStruct((8, 2048), BF16),
        compiler_params=SMALL,
        cost_estimate=pl.CostEstimate(flops=2**20, bytes_accessed=2**20, transcendentals=0),
        name="gather",
    )(*blocks)


def assemble_kernel(b0, b1, b2, b3, weight_ref):
    x = here("x")
    for step, ref in enumerate((b0, b1, b2, b3)):
        row = pl.multiple_of(8 * lax.rem(x - step + 4, 4), 8)
        weight_ref[pl.ds(row, 8), :] = ref[...].astype(F32)


def assemble(blocks):
    vmem = pl.BlockSpec(memory_space=pltpu.VMEM)
    return pl.pallas_call(
        assemble_kernel,
        in_specs=[vmem] * 4,
        out_specs=vmem,
        out_shape=jax.ShapeDtypeStruct((32, 2048), F32),
        compiler_params=SMALL,
        name="assemble",
    )(*blocks)


def along(block, axis, step):
    size = lax.axis_size(axis)
    return lax.ppermute(block, axis, [(i, (i + step) % size) for i in range(size)])


def around(block, step, other):
    route = [(2 * i + c, 2 * ((i + step) % 4) + (c ^ other)) for i in range(4) for c in range(2)]
    return lax.ppermute(block, ("x", "c"), route)


def body(inputs, cotangent, lengths, angles, mix, weight):
    x, cot = inputs[0], cotangent[0]
    seq = ("z", "y", "c")
    factor = float(4 * 8192) ** (-0.5)

    def exchange(block):
        return lax.all_to_all(block, seq, split_axis=0, concat_axis=0, tiled=True)

    act_grad = dot(cot, weight, ((1,), (1,))).astype(BF16)
    got = exchange(pack(x, act_grad))
    cots = [cot] + [along(cot, "x", step) for step in (1, 2, 3)]

    coef = lax.dynamic_slice_in_dim(
        jnp.concatenate([angles, mix], axis=0), 32 * lax.axis_index(seq), 32, axis=1
    )
    coef = jnp.tile(coef, (1, 4))

    got, cots = lax.optimization_barrier((got, cots))
    cots = cots + [around(block, 0, 1) for block in cots]
    act, keep = forward(lengths, coef, got)
    got_act = exchange(act)
    done, tail = backward(lengths, coef, keep)
    done, tail, cots, got_act = lax.optimization_barrier((done, tail, cots, got_act))

    sends = to_send(got_act, tail)
    acts = [
        sends[at] if at == 0 else around(sends[at], at % 4, at // 4) for at in range(8)
    ]
    done = merge(done, acts[:4])
    parts = outer(acts, cots)
    output = jnp.dot(natural_act(got_act), weight, preferred_element_type=F32).astype(BF16)
    parts = [parts[0]] + [along(parts[step], "y", step) for step in (1, 2, 3)]
    got_done = exchange(done)
    parts = add_four(parts)
    parts = [parts[0]] + [along(parts[step], "z", step) for step in range(1, 8)]
    input_grad, angle_grad, mix_grad = natural_grad(got_done, factor)
    block = gather(parts, factor)
    weight_grad = assemble([block] + [along(block, "x", step) for step in (1, 2, 3)])
    return output[None], input_grad[None], weight_grad, angle_grad, mix_grad


def solution(mesh):
    grid = Mesh(mesh.devices.reshape(4, 8, 4, 2), ("x", "z", "y", "c"))
    seq = ("z", "y", "c")
    split = P("x", seq, None)
    in_specs = (split, split, P("x", None), P(), P(), P())
    out_specs = (split, split, P(seq, None), P(), P())
    return jax.shard_map(body, mesh=grid, in_specs=in_specs, out_specs=out_specs, check_vma=False)
```

```python
import functools
import math

import jax
import jax.numpy as jnp
from jax import lax
from jax.experimental import pallas as pl
from jax.experimental.pallas import tpu as pltpu
from jax.sharding import Mesh
from jax.sharding import PartitionSpec as P


F32 = jnp.float32
BF16 = jnp.bfloat16
ROWS = 2048
PAD = 1024
LEVELS = 13
CHUNK = 512
GELU_K = math.sqrt(2.0 / math.pi)
LARGE = pltpu.CompilerParams(vmem_limit_bytes=52 << 20)
SMALL = pltpu.CompilerParams(vmem_limit_bytes=12 << 20)


def swap_groups(tiles, width):
    count = len(tiles)
    lane = lax.broadcasted_iota(jnp.int32, tiles[0].shape, 1)
    bit = 1
    while bit < count:
        high = (lane // width) & bit != 0
        new = list(tiles)
        for t in range(count):
            if t & bit == 0:
                a, b = tiles[t], tiles[t | bit]
                new[t] = jnp.where(high, pltpu.roll(b, bit * width, 1), a)
                new[t | bit] = jnp.where(high, b, pltpu.roll(a, 128 - bit * width, 1))
        tiles = new
        bit *= 2
    return tiles


def row_order(inverse):
    i = lax.broadcasted_iota(jnp.int32, (128, 128), 0)
    k = lax.broadcasted_iota(jnp.int32, (128, 128), 1)
    if inverse:
        i, k = k, i
    return (k == 4 * (i % 32) + i // 32).astype(F32).astype(BF16)


def dot(a, b, dims):
    return lax.dot_general(a, b, (dims, ((), ())), preferred_element_type=F32)


def pack_kernel(x_ref, grad_ref, out_ref):
    order = row_order(False)
    for at, block in ((0, x_ref), (32, grad_ref)):
        ordered = dot(order, block[...], ((1,), (0,)))
        for tile in range(block.shape[1] // 128):
            part = [ordered[32 * q : 32 * q + 32, 128 * tile : 128 * tile + 128] for q in range(4)]
            for jj, value in enumerate(swap_groups(part, 32)):
                out_ref[4 * tile + jj, at : at + 32, :] = value.astype(BF16)


def pack(x, act_grad):
    width = 1024
    part = pl.BlockSpec((128, width), lambda n: (0, n))
    return pl.pallas_call(
        pack_kernel,
        grid=(2048 // width,),
        in_specs=[part, part],
        out_specs=pl.BlockSpec((width // 32, 64, 128), lambda n: (n, 0, 0)),
        out_shape=jax.ShapeDtypeStruct((64, 64, 128), BF16),
        compiler_params=SMALL,
        cost_estimate=pl.CostEstimate(flops=10**8, bytes_accessed=2**21, transcendentals=0),
        name="pack",
    )(x, act_grad)


def filters(coef_ref):
    cos_a, sin_a = jnp.cos(coef_ref[0:1, :]), jnp.sin(coef_ref[0:1, :])
    cos_d, sin_d = jnp.cos(coef_ref[1:2, :]), jnp.sin(coef_ref[1:2, :])
    mix = [coef_ref[2 + level : 3 + level, :] for level in range(LEVELS + 1)]
    return cos_a, sin_a, cos_d, sin_d, mix


def positions(len_ref, r0):
    row = lax.broadcasted_iota(jnp.int32, (CHUNK, 128), 0)
    lane = lax.broadcasted_iota(jnp.int32, (CHUNK, 128), 1)
    time = 4 * (r0 + row) + lane // 32
    start = jnp.zeros((CHUNK, 128), jnp.int32)
    end = jnp.int32(0)
    for s in range(4):
        length = len_ref[0, s]
        end = end + length
        start = start + jnp.where(end <= time, length, 0)
    return time - start


def forward_kernel(len_ref, coef_ref, in_ref, act_ref, keep_ref, a_ref, pos_ref, mixed_ref, sems):
    lane = lax.broadcasted_iota(jnp.int32, (CHUNK, 128), 1)
    cos_a, sin_a, cos_d, sin_d, mix = filters(coef_ref)
    sources = CHUNK // 32

    def start_up(n, carry):
        r0 = pl.multiple_of(n * CHUNK, CHUNK)
        pos_ref[pl.ds(r0, CHUNK), :] = positions(len_ref, r0)
        got = in_ref[pl.ds(n * sources, sources), 0:32, :].astype(F32)
        a_ref[0, pl.ds(PAD + r0, CHUNK), :] = got.reshape(CHUNK, 128)
        return carry

    def save(level):
        return pltpu.make_async_copy(
            a_ref.at[level, pl.ds(PAD, ROWS)], keep_ref.at[level], sems.at[level]
        )

    lax.fori_loop(0, ROWS // CHUNK, start_up, 0)
    save(0).start()

    def behind(level, r0):
        dist = 2**level
        if dist >= 4:
            moved = a_ref[level, pl.ds(PAD + r0 - dist // 4, CHUNK), :]
        else:
            here = a_ref[level, pl.ds(PAD + r0, CHUNK), :]
            before = a_ref[level, pl.ds(PAD + r0 - 1, CHUNK), :]
            moved = pltpu.roll(jnp.where(lane >= 128 - 32 * dist, before, here), 32 * dist, 1)
        return jnp.where(pos_ref[pl.ds(r0, CHUNK), :] >= dist, moved, 0.0)

    for level in range(LEVELS):
        to_mix = mix[level] * cos_d
        to_mix_s = mix[level] * sin_d

        def step(n, carry, level=level, to_mix=to_mix, to_mix_s=to_mix_s):
            r0 = pl.multiple_of(n * CHUNK, CHUNK)
            rows = pl.ds(r0, CHUNK)
            plain = a_ref[level, pl.ds(PAD + r0, CHUNK), :]
            shifted = behind(level, r0)
            term = to_mix * plain + to_mix_s * shifted
            mixed = term if level == 0 else mixed_ref[rows, :] + term
            above = cos_a * plain + sin_a * shifted
            a_ref[level + 1, pl.ds(PAD + r0, CHUNK), :] = above
            if level == LEVELS - 1:
                mixed = mixed + mix[LEVELS] * above
                th = jnp.tanh(GELU_K * (mixed + 0.044715 * (mixed * mixed * mixed)))
                half = 0.5 * (1.0 + th)
                tail = 0.5 * mixed * (1.0 - th * th)
                slope = half + tail * (GELU_K * (1.0 + 3 * 0.044715 * (mixed * mixed)))
                blocks = pl.ds(n * sources, sources)
                act_ref[blocks] = (mixed * half).astype(BF16).reshape(sources, 32, 128)
                act_grad = in_ref[blocks, 32:64, :].astype(F32).reshape(CHUNK, 128)
                mixed = (slope * act_grad).astype(BF16).astype(F32)
            mixed_ref[rows, :] = mixed
            return carry

        lax.fori_loop(0, ROWS // CHUNK, step, 0)
        save(level + 1).start()
    last = pltpu.make_async_copy(mixed_ref, keep_ref.at[LEVELS + 1], sems.at[LEVELS + 1])
    last.start()
    for level in range(LEVELS + 1):
        save(level).wait()
    last.wait()


def forward(lengths, coef, received):
    vmem = pl.BlockSpec(memory_space=pltpu.VMEM)
    return pl.pallas_call(
        forward_kernel,
        in_specs=[pl.BlockSpec(memory_space=pltpu.SMEM), vmem, vmem],
        out_specs=[vmem, pl.BlockSpec(memory_space=pltpu.HBM)],
        out_shape=[
            jax.ShapeDtypeStruct((64, 32, 128), BF16),
            jax.ShapeDtypeStruct((LEVELS + 2, ROWS, 128), F32),
        ],
        scratch_shapes=[
            pltpu.VMEM((LEVELS + 1, PAD + ROWS, 128), F32),
            pltpu.VMEM((ROWS, 128), jnp.int32),
            pltpu.VMEM((ROWS, 128), F32),
            pltpu.SemaphoreType.DMA((LEVELS + 2,)),
        ],
        compiler_params=LARGE,
        cost_estimate=pl.CostEstimate(flops=10**8, bytes_accessed=2**25, transcendentals=2**18),
        name="forward",
    )(lengths, coef, received)


def backward_kernel(len_ref, coef_ref, keep_ref, out_ref, a_ref, pos_ref, g_ref, u_ref, sum_ref, sems):
    lane = lax.broadcasted_iota(jnp.int32, (CHUNK, 128), 1)
    cos_a, sin_a, cos_d, sin_d, mix = filters(coef_ref)
    sources = CHUNK // 32

    def load(level):
        return pltpu.make_async_copy(keep_ref.at[level], a_ref.at[level], sems.at[level])

    first = pltpu.make_async_copy(
        keep_ref.at[LEVELS + 1], g_ref.at[pl.ds(0, ROWS)], sems.at[LEVELS + 1]
    )
    first.start()
    for level in reversed(range(LEVELS + 1)):
        load(level).start()

    def fold(value):
        return jnp.sum(value.reshape(CHUNK // 8, 8, 128), axis=0)

    def over_q(value):
        row = jnp.sum(value, axis=0, keepdims=True)
        row = row + pltpu.roll(row, 32, 1)
        return row + pltpu.roll(row, 64, 1)

    zero = jnp.zeros((8, 128), F32)
    first.wait()
    load(LEVELS).wait()

    def start_up(n, carry):
        r0 = pl.multiple_of(n * CHUNK, CHUNK)
        rows = pl.ds(r0, CHUNK)
        pos_ref[rows, :] = positions(len_ref, r0)
        g = g_ref[rows, :]
        u_ref[1, rows, :] = mix[LEVELS] * g
        return carry + fold(g * a_ref[LEVELS, rows, :])

    sum_ref[15:16, :] = over_q(lax.fori_loop(0, ROWS // CHUNK, start_up, zero))
    pos_ref[pl.ds(ROWS, PAD), :] = jnp.full((PAD, 128), -1, jnp.int32)

    sum_ua, sum_us = zero, zero
    phi = jnp.zeros((1, 128), F32)
    for level in reversed(range(LEVELS)):
        dist = 2**level
        source, target = (1, 0) if level % 2 == 0 else (0, 1)
        from_g = mix[level] * cos_d
        from_g_s = mix[level] * sin_d
        load(level).wait()

        def step(n, carry, level=level, dist=dist, source=source, target=target, from_g=from_g, from_g_s=from_g_s):
            ua, us, ga, gs = carry
            r0 = pl.multiple_of(n * CHUNK, CHUNK)
            rows = pl.ds(r0, CHUNK)
            u, g = u_ref[source, rows, :], g_ref[rows, :]
            if dist >= 4:
                later = pl.ds(r0 + dist // 4, CHUNK)
                u_on, g_on, pos = u_ref[source, later, :], g_ref[later, :], pos_ref[later, :]
            else:
                later = pl.ds(r0 + 1, CHUNK)

                def ahead(here, there):
                    return pltpu.roll(jnp.where(lane < 32 * dist, there, here), 128 - 32 * dist, 1)

                u_on = ahead(u, u_ref[source, later, :])
                g_on = ahead(g, g_ref[later, :])
                pos = ahead(pos_ref[rows, :], pos_ref[later, :])
            keep = pos >= dist
            u_on = jnp.where(keep, u_on, 0.0)
            g_on = jnp.where(keep, g_on, 0.0)
            new = (cos_a * u + from_g * g) + (sin_a * u_on + from_g_s * g_on)
            plain = a_ref[level, rows, :]
            if level > 0:
                u_ref[target, rows, :] = new
            else:
                blocks = pl.ds(n * sources, sources)
                out_ref[blocks, 0:32, :] = new.astype(BF16).reshape(sources, 32, 128)
            return (
                ua + fold(u * plain),
                us + fold(u_on * plain),
                ga + fold(g * plain),
                gs + fold(g_on * plain),
            )

        sum_ua, sum_us, ga, gs = lax.fori_loop(
            0, ROWS // CHUNK, step, (sum_ua, sum_us, zero, zero)
        )
        ga, gs = over_q(ga), over_q(gs)
        sum_ref[2 + level : 3 + level, :] = cos_d * ga + sin_d * gs
        phi = phi + mix[level] * (cos_d * gs - sin_d * ga)
    sum_ref[0:1, :] = cos_a * over_q(sum_us) - sin_a * over_q(sum_ua)
    sum_ref[1:2, :] = phi
    group = lax.broadcasted_iota(jnp.int32, (4, 128), 1) // 32
    packed = jnp.zeros((4, 128), F32)
    for b in range(4):
        packed = jnp.where(group == b, sum_ref[4 * b : 4 * b + 4, :], packed)
    high = packed.astype(BF16).astype(F32)
    both = jnp.concatenate([high, packed - high], axis=0).astype(BF16)
    out_ref[:, 32:40, :] = jnp.broadcast_to(both[None], (64, 8, 128))


def backward(lengths, coef, keep):
    vmem = pl.BlockSpec(memory_space=pltpu.VMEM)
    return pl.pallas_call(
        backward_kernel,
        in_specs=[
            pl.BlockSpec(memory_space=pltpu.SMEM), vmem, pl.BlockSpec(memory_space=pltpu.HBM),
        ],
        out_specs=vmem,
        out_shape=jax.ShapeDtypeStruct((64, 40, 128), BF16),
        scratch_shapes=[
            pltpu.VMEM((LEVELS + 1, ROWS, 128), F32),
            pltpu.VMEM((ROWS + PAD, 128), jnp.int32),
            pltpu.VMEM((ROWS + PAD, 128), F32),
            pltpu.VMEM((2, ROWS + PAD, 128), F32),
            pltpu.VMEM((16, 128), F32),
            pltpu.SemaphoreType.DMA((LEVELS + 2,)),
        ],
        compiler_params=LARGE,
        cost_estimate=pl.CostEstimate(flops=10**8, bytes_accessed=2**25, transcendentals=2**18),
        name="backward",
    )(lengths, coef, keep)


def natural(in_ref, out_ref, order, tile):
    part = [in_ref[4 * tile + jj, 0:32, :].astype(F32) for jj in range(4)]
    rows = jnp.concatenate(swap_groups(part, 32), axis=0).astype(BF16)
    lanes = slice(128 * tile, 128 * tile + 128)
    out_ref[:, lanes] = dot(order, rows, ((1,), (0,))).astype(BF16)


def act_kernel(in_ref, act_ref):
    order = row_order(True)
    for tile in range(16):
        natural(in_ref, act_ref, order, tile)


def natural_act(received):
    vmem = pl.BlockSpec(memory_space=pltpu.VMEM)
    return pl.pallas_call(
        act_kernel,
        in_specs=[vmem],
        out_specs=vmem,
        out_shape=jax.ShapeDtypeStruct((128, 2048), BF16),
        cost_estimate=pl.CostEstimate(flops=10**8, bytes_accessed=2**20, transcendentals=0),
        compiler_params=SMALL,
        name="natural_act",
    )(received)


def grad_kernel(in_ref, grad_ref, sums_ref):
    order = row_order(True)
    for tile in range(16):
        natural(in_ref, grad_ref, order, tile)
        part = []
        for jj in range(4):
            both = in_ref[4 * tile + jj, 32:40, :].astype(F32)
            part.append(both[0:4] + both[4:8])
        for b, value in enumerate(swap_groups(part, 32)):
            sums_ref[4 * b : 4 * b + 4, 128 * tile : 128 * tile + 128] = value


def natural_grad(received):
    vmem = pl.BlockSpec(memory_space=pltpu.VMEM)
    return pl.pallas_call(
        grad_kernel,
        in_specs=[vmem],
        out_specs=[vmem] * 2,
        out_shape=[
            jax.ShapeDtypeStruct((128, 2048), BF16),
            jax.ShapeDtypeStruct((16, 2048), F32),
        ],
        cost_estimate=pl.CostEstimate(flops=10**8, bytes_accessed=2**20, transcendentals=0),
        compiler_params=SMALL,
        name="natural_grad",
    )(received)


def send_kernel(place_ref, in_ref, *refs):
    outs, send_ref = refs[:8], refs[8]
    x, c = place_ref[0], place_ref[1]
    for half in range(2):
        for core in range(2):
            other = jnp.where(c == core, 0, 4)
            for chunk in range(2):
                part = []
                for y in (2 * half, 2 * half + 1):
                    for z in range(8):
                        source = 8 * z + 2 * y + core
                        part.append(in_ref[source, 16 * chunk : 16 * chunk + 16, :].astype(F32))
                for at, value in enumerate(swap_groups(part, 8)):
                    q, to = at // 4, at % 4
                    row = 32 * q + 16 * chunk
                    slot = other + lax.rem(to - x + 4, 4)
                    send_ref[slot, row : row + 16, 128 * half : 128 * half + 128] = value.astype(BF16)
    for slot in range(8):
        outs[slot][...] = send_ref[slot]


def to_send(place, received):
    vmem = pl.BlockSpec(memory_space=pltpu.VMEM)
    return pl.pallas_call(
        send_kernel,
        in_specs=[pl.BlockSpec(memory_space=pltpu.SMEM), vmem],
        out_specs=[vmem] * 8,
        out_shape=[jax.ShapeDtypeStruct((128, 256), BF16)] * 8,
        scratch_shapes=[pltpu.VMEM((8, 128, 256), BF16)],
        cost_estimate=pl.CostEstimate(flops=10**8, bytes_accessed=2**20, transcendentals=0),
        compiler_params=SMALL,
        name="to_send",
    )(place, received)


def outer_kernel(place_ref, *refs):
    acts, cots, outs, act_ref = refs[:8], refs[8:16], refs[16:20], refs[20]

    @pl.when(pl.program_id(0) == 0)
    def _():
        order = row_order(False)
        for at in range(8):
            act = dot(acts[at][...], order, ((0,), (0,))).astype(BF16)
            for y in range(4):
                slot = lax.rem(y - place_ref[2] + 4, 4)
                act_ref[slot, :, 128 * at : 128 * at + 128] = act[64 * y : 64 * y + 64]

    together = jnp.concatenate([ref[...] for ref in cots], axis=0)
    total = dot(act_ref[...].reshape(256, 1024), together, ((1,), (0,))).astype(BF16)
    for slot in range(4):
        outs[slot][...] = total[64 * slot : 64 * slot + 64]


def outer(place, acts, cots):
    width = 512
    whole = pl.BlockSpec((128, 256), lambda n: (0, 0))
    part = pl.BlockSpec((128, width), lambda n: (0, n))
    return pl.pallas_call(
        outer_kernel,
        grid=(2048 // width,),
        in_specs=[pl.BlockSpec(memory_space=pltpu.SMEM)] + [whole] * 8 + [part] * 8,
        out_specs=[pl.BlockSpec((64, width), lambda n: (0, n))] * 4,
        out_shape=[jax.ShapeDtypeStruct((64, 2048), BF16)] * 4,
        scratch_shapes=[pltpu.VMEM((4, 64, 1024), BF16)],
        cost_estimate=pl.CostEstimate(flops=2**30, bytes_accessed=2**23, transcendentals=0),
        name="outer",
    )(place, *acts, *cots)


def add_kernel(place_ref, b0, b1, b2, b3, *refs):
    outs, total_ref = refs[:8], refs[8]
    total_ref[...] = (b0[...].astype(F32) + b1[...].astype(F32)) + (b2[...].astype(F32) + b3[...].astype(F32))
    for step in range(8):
        row = pl.multiple_of(8 * lax.rem(place_ref[3] + step, 8), 8)
        outs[step][...] = total_ref[pl.ds(row, 8), :].astype(BF16)


def add_four(place, blocks):
    vmem = pl.BlockSpec(memory_space=pltpu.VMEM)
    return pl.pallas_call(
        add_kernel,
        in_specs=[pl.BlockSpec(memory_space=pltpu.SMEM)] + [vmem] * 4,
        out_specs=[vmem] * 8,
        out_shape=[jax.ShapeDtypeStruct((8, 2048), BF16)] * 8,
        scratch_shapes=[pltpu.VMEM((64, 2048), F32)],
        compiler_params=SMALL,
        cost_estimate=pl.CostEstimate(flops=2**20, bytes_accessed=2**20, transcendentals=0),
        name="add_four",
    )(place, *blocks)


def gather_kernel(*refs, factor):
    blocks, sums_ref, out_ref = refs[:8], refs[8], refs[9]
    total = blocks[0][...].astype(F32)
    for ref in blocks[1:]:
        total = total + ref[...].astype(F32)
    out_ref[0:8, :] = (total * factor).astype(BF16)
    out_ref[8:24, :] = (sums_ref[...] * factor).astype(BF16)


def gather(blocks, sums, factor):
    vmem = pl.BlockSpec(memory_space=pltpu.VMEM)
    return pl.pallas_call(
        functools.partial(gather_kernel, factor=factor),
        in_specs=[vmem] * 9,
        out_specs=vmem,
        out_shape=jax.ShapeDtypeStruct((24, 2048), BF16),
        compiler_params=SMALL,
        cost_estimate=pl.CostEstimate(flops=2**20, bytes_accessed=2**20, transcendentals=0),
        name="gather",
    )(*blocks, sums)


def assemble_kernel(place_ref, b0, b1, b2, b3, weight_ref, angle_ref, mix_ref, sums_ref):
    x = place_ref[0]
    for step, ref in enumerate((b0, b1, b2, b3)):
        source = lax.rem(x - step + 4, 4)
        block = ref[...].astype(F32)
        weight_ref[pl.ds(pl.multiple_of(8 * source, 8), 8), :] = block[0:8]
        sums_ref[source] = block[8:24]
    total = (sums_ref[0] + sums_ref[1]) + (sums_ref[2] + sums_ref[3])
    angle_ref[...] = total[0:2]
    mix_ref[...] = total[2:16]


def assemble(place, blocks):
    vmem = pl.BlockSpec(memory_space=pltpu.VMEM)
    return pl.pallas_call(
        assemble_kernel,
        in_specs=[pl.BlockSpec(memory_space=pltpu.SMEM)] + [vmem] * 4,
        out_specs=[vmem] * 3,
        out_shape=[
            jax.ShapeDtypeStruct((32, 2048), F32),
            jax.ShapeDtypeStruct((2, 2048), F32),
            jax.ShapeDtypeStruct((14, 2048), F32),
        ],
        scratch_shapes=[pltpu.VMEM((4, 16, 2048), F32)],
        compiler_params=SMALL,
        name="assemble",
    )(place, *blocks)


def along(block, axis, step):
    size = lax.axis_size(axis)
    return lax.ppermute(block, axis, [(i, (i + step) % size) for i in range(size)])


def around(block, step, other):
    route = [(2 * i + c, 2 * ((i + step) % 4) + (c ^ other)) for i in range(4) for c in range(2)]
    return lax.ppermute(block, ("x", "c"), route)


def body(inputs, cotangent, lengths, angles, mix, weight):
    x, cot = inputs[0], cotangent[0]
    seq = ("z", "y", "c")
    place = jnp.stack([lax.axis_index(name) for name in ("x", "c", "y", "z")]).astype(jnp.int32)
    factor = float(4 * 8192) ** (-0.5)

    def exchange(block):
        return lax.all_to_all(block, seq, split_axis=0, concat_axis=0, tiled=True)

    act_grad = dot(cot, weight, ((1,), (1,))).astype(BF16)
    got = exchange(pack(x, act_grad))
    cots = [cot] + [along(cot, "x", step) for step in (1, 2, 3)]

    coef = lax.dynamic_slice_in_dim(
        jnp.concatenate([angles, mix], axis=0), 32 * lax.axis_index(seq), 32, axis=1
    )
    coef = jnp.tile(coef, (1, 4))

    got, cots = lax.optimization_barrier((got, cots))
    cots = cots + [around(block, 0, 1) for block in cots]
    act, keep = forward(lengths, coef, got)
    got_act = exchange(act)
    done = backward(lengths, coef, keep)
    done, cots, got_act = lax.optimization_barrier((done, cots, got_act))

    got_done = exchange(done)
    sends = to_send(place, got_act)
    acts = [
        sends[at] if at == 0 else around(sends[at], at % 4, at // 4) for at in range(8)
    ]
    parts = outer(place, acts, cots)
    output = jnp.dot(natural_act(got_act), weight, preferred_element_type=F32).astype(BF16)
    parts = [parts[0]] + [along(parts[step], "y", step) for step in (1, 2, 3)]
    parts, output = lax.optimization_barrier((parts, output))
    parts = add_four(place, parts)
    parts = [parts[0]] + [along(parts[step], "z", step) for step in range(1, 8)]
    input_grad, sums = natural_grad(got_done)
    block = gather(parts, sums, factor)
    weight_grad, angle_grad, mix_grad = assemble(
        place, [block] + [along(block, "x", step) for step in (1, 2, 3)]
    )
    return output[None], input_grad[None], weight_grad, angle_grad, mix_grad


def solution(mesh):
    grid = Mesh(mesh.devices.reshape(4, 8, 4, 2), ("x", "z", "y", "c"))
    seq = ("z", "y", "c")
    split = P("x", seq, None)
    in_specs = (split, split, P("x", None), P(), P(), P())
    out_specs = (split, split, P(seq, None), P(), P())
    return jax.shard_map(body, mesh=grid, in_specs=in_specs, out_specs=out_specs, check_vma=False)
```
